32 devices in a mesh: gx: 4 (over y, x), gy: 2 (over core), gz: 4 (over z).
Axes of the slice: x: 2, y: 2, z: 4, core: 2. Of those that a mesh axis runs over, the one named last changes fastest.
Arguments:
- flow_state: float32 [4, 16, 64, 512], P(None, 'gx', 'gy', 'gz'), may hold values from -6 to 6
- viscosity: float32 [4, 16, 64, 512], P(None, 'gx', 'gy', 'gz'), may hold values from 0.05 to 0.5
- lift_weight: float32 [8, 128], replicated, may hold values from -6 to 6
- lift_bias: float32 [128], replicated, may hold values from -2 to 2
- norm_gains: float32 [6, 128], replicated, may hold values from 0.1 to 1.9
- query_weight: bfloat16 [2, 128, 128], replicated, may hold values from -4 to 4
- key_weight: bfloat16 [2, 128, 128], replicated, may hold values from -4 to 4
- value_weight: bfloat16 [2, 128, 128], replicated, may hold values from -0.5 to 0.5
- output_weight: bfloat16 [2, 128, 128], replicated, may hold values from -0.5 to 0.5
- up_weight: bfloat16 [2, 128, 512], replicated, may hold values from -0.5 to 0.5
- down_weight: bfloat16 [2, 512, 128], replicated, may hold values from -0.25 to 0.25
- head_weight: bfloat16 [128, 4], replicated, may hold values from -1.5 to 1.5
Outputs:
- state_next: float32 [4, 16, 64, 512], P(None, 'gx', 'gy', 'gz')
- eddy_field: float32 [4, 16, 64, 512], P(None, 'gx', 'gy', 'gz')
The draws below stay inside these ranges and needn't reach their ends.
All inputs are finite; a program needn't handle non-finite values.
Results may differ from the reference program's by a relative error of at most 0.0058.
The reference program's roundings to bfloat16 on the way count: a program that leaves them out, or rounds other values in their place, can miss the bound.
Values may be sent and summed in bfloat16 or wider, within the bound.
No kernel may reach another device: no remote copies, remote signals or barrier semaphores. Data moves between devices by JAX's collectives and lax.ppermute only.
A program may use at most 64 MiB of HBM per device.

```python
import math
import jax
import jax.numpy as jnp
from jax import lax

FIELDS = 4
D = 128
HID = 512
NX = 16
NY = 64
NZ = 512


def draw_query_weight(key, part):
    private_part = jax.random.normal(jax.random.fold_in(key, 1), (2, D, D), jnp.float32) * D ** (-0.5)
    return jnp.clip(private_part, -4.0, 4.0).astype(jnp.bfloat16)


def draw_key_weight(key, part):
    private_part = jax.random.normal(jax.random.fold_in(key, 2), (2, D, D), jnp.float32) * D ** (-0.5)
    return jnp.clip(private_part, -4.0, 4.0).astype(jnp.bfloat16)


def block_scale(key, shape, split, least, high):
    level, own = 1.0, jax.random.fold_in(key, 6)
    for dim, parts in split:
        steps = jnp.exp(jax.random.uniform(jax.random.fold_in(own, dim), (parts,), jnp.float32, least / len(split), high / len(split)))
        level = level * jnp.repeat(steps, shape[dim] // parts).reshape([-1 if axis == dim else 1 for axis in range(len(shape))])
    return level


def centred(stream_key, shape, scale, most, split=(), kind=jnp.bfloat16):
    level = block_scale(stream_key, shape, split, -0.22, 0.18) if split else 1.0
    drawn = jax.random.normal(stream_key, shape, jnp.float32) * scale * level
    return jnp.minimum(jnp.maximum(drawn, -most), most).astype(kind)


def setup_inputs(seed: int = 0) -> dict:
    splits = jax.random.split(jax.random.key(seed), 13)
    flow_state = centred(splits[0], (FIELDS, NX, NY, NZ), 1.0, 6.0, ((1, 4), (2, 2), (3, 4)), jnp.float32)
    viscosity = jnp.clip(jnp.exp(math.log(0.5) - 2.3025851 * jax.random.uniform(splits[1], (FIELDS, NX, NY, NZ), jnp.float32) ** block_scale(splits[1], (FIELDS, NX, NY, NZ), ((1, 4), (2, 2), (3, 4)), -0.2, 0.2)), 0.05, 0.5)
    lift_weight = centred(splits[2], (2 * FIELDS, D), 1 ** -0.5, 6.0, (), jnp.float32)
    lift_bias = centred(splits[3], (D,), 0.5, 2.0, (), jnp.float32)
    norm_gains = jnp.clip(1.0 + 0.18 * jax.random.normal(splits[4], (6, D), jnp.float32), 0.1, 1.9)
    query_weight = draw_query_weight(jax.random.fold_in(splits[12], 71), 0)
    key_weight = draw_key_weight(jax.random.fold_in(splits[12], 71), 0)
    value_weight = centred(splits[7], (2, D, D), D ** -0.5, 0.5)
    output_weight = centred(splits[8], (2, D, D), D ** -0.5, 0.5)
    up_weight = centred(splits[9], (2, D, HID), D ** -0.5, 0.5)
    down_weight = centred(splits[10], (2, HID, D), HID ** -0.5, 0.25)
    head_weight = centred(splits[11], (D, FIELDS), (D // 8) ** -0.5, 1.5)
    return dict(flow_state=flow_state, viscosity=viscosity, lift_weight=lift_weight, lift_bias=lift_bias, norm_gains=norm_gains, query_weight=query_weight, key_weight=key_weight, value_weight=value_weight, output_weight=output_weight, up_weight=up_weight, down_weight=down_weight, head_weight=head_weight)


EPSILON = 1e-06
TIME_STEP = 0.3

def window(source, which_axis, offset):
    slicers = [slice(None), slice(1, -1), slice(1, -1), slice(1, -1)]
    slicers[which_axis] = slice(1 + offset, source.shape[which_axis] - 1 + offset)
    return source[tuple(slicers)]

def tendency(fields, viscous):
    middle = window(fields, 1, 0)
    nu_middle = window(viscous, 1, 0)
    summed = jnp.zeros_like(middle)
    for which_axis in (1, 2, 3):
        forward = window(fields, which_axis, 1)
        backward = window(fields, which_axis, -1)
        nu_forward = 0.5 * (nu_middle + window(viscous, which_axis, 1))
        nu_backward = 0.5 * (nu_middle + window(viscous, which_axis, -1))
        velocity = middle[which_axis - 1][None]
        summed = summed - velocity * (0.5 * (forward - backward)) + nu_forward * (forward - middle) - nu_backward * (middle - backward)
    return summed

def periodic(source):
    return jnp.pad(source, ((0, 0), (1, 1), (1, 1), (1, 1)), mode='wrap')

def coarsen(source):
    shaped = source.reshape(source.shape[0], source.shape[1] // 2, 2, source.shape[2] // 2, 2, source.shape[3] // 2, 2)
    return lax.optimization_barrier(jnp.mean(shaped, axis=(2, 4, 6)))

def refine(padded, which_axis):
    extent = padded.shape[which_axis]
    center = lax.slice_in_dim(padded, 1, extent - 1, axis=which_axis)
    behind = lax.slice_in_dim(padded, 0, extent - 2, axis=which_axis)
    forward = lax.slice_in_dim(padded, 2, extent, axis=which_axis)
    lower_half = 0.75 * center + 0.25 * behind
    upper_half = 0.75 * center + 0.25 * forward
    paired = jnp.stack([lower_half, upper_half], axis=which_axis + 1)
    new_shape = list(center.shape)
    new_shape[which_axis] = 2 * new_shape[which_axis]
    return paired.reshape(new_shape)

def rms_scale(values, scaling):
    return values * lax.rsqrt(lax.optimization_barrier(jnp.mean(values * values, axis=-1, keepdims=True)) + EPSILON) * scaling

def matmul(values, matrix):
    flat_rows = values.reshape(-1, values.shape[-1])
    product = jnp.dot(flat_rows, matrix, preferred_element_type=jnp.float32)
    return product.reshape(values.shape[:-1] + (matrix.shape[-1],))

def mixer(section, along_axis, weights, gain_pair):
    query_matrix, key_matrix, value_matrix, output_matrix, up_matrix, down_matrix = weights
    carried = section.astype(jnp.float32)
    normed = rms_scale(carried, gain_pair[0]).astype(jnp.bfloat16)
    queries = matmul(normed, query_matrix).astype(jnp.bfloat16)
    key_rows = matmul(normed, key_matrix).astype(jnp.bfloat16)
    value_rows = matmul(normed, value_matrix).astype(jnp.bfloat16)
    if along_axis == 0:
        scores = jnp.einsum('lnd,mnd->nlm', queries.astype(jnp.float32), key_rows.astype(jnp.float32))
    else:
        scores = jnp.einsum('nld,nmd->nlm', queries.astype(jnp.float32), key_rows.astype(jnp.float32))
    scores = scores * queries.shape[-1] ** (-0.5)
    scores = scores - lax.optimization_barrier(jnp.max(scores, axis=-1, keepdims=True))
    exponent = jnp.exp(scores)
    attention = (exponent / lax.optimization_barrier(jnp.sum(exponent, axis=-1, keepdims=True))).astype(jnp.bfloat16)
    if along_axis == 0:
        attended = jnp.einsum('nlm,mnd->lnd', attention.astype(jnp.float32), value_rows.astype(jnp.float32))
    else:
        attended = jnp.einsum('nlm,nmd->nld', attention.astype(jnp.float32), value_rows.astype(jnp.float32))
    attended = attended.astype(jnp.bfloat16)
    residual = carried + matmul(attended, output_matrix)
    normed_again = rms_scale(residual, gain_pair[1]).astype(jnp.bfloat16)
    hidden = jax.nn.gelu(matmul(normed_again, up_matrix)).astype(jnp.bfloat16)
    return (residual + matmul(hidden, down_matrix)).astype(jnp.bfloat16)

def advance(flow_state, viscosity):
    viscous_wide = periodic(viscosity)
    segment_one = flow_state + TIME_STEP * tendency(periodic(flow_state), viscous_wide)
    segment_two = 0.75 * flow_state + 0.25 * (segment_one + TIME_STEP * tendency(periodic(segment_one), viscous_wide))
    return flow_state / 3.0 + 2.0 / 3.0 * (segment_two + TIME_STEP * tendency(periodic(segment_two), viscous_wide))

def reference(flow_state, viscosity, lift_weight, lift_bias, norm_gains, query_weight, key_weight, value_weight, output_weight, up_weight, down_weight, head_weight):
    state_next = advance(flow_state, viscosity)
    filtered = jnp.concatenate([coarsen(state_next), coarsen(state_next * state_next)], axis=0)
    channels, first_extent, second_extent, third_extent = filtered.shape
    group_size = math.gcd(third_extent, 4)
    grouped = filtered.reshape(channels, first_extent, second_extent, third_extent // group_size, group_size)
    grouped = jnp.transpose(grouped, (3, 0, 1, 4, 2))
    first_weights = (query_weight[0], key_weight[0], value_weight[0], output_weight[0], up_weight[0], down_weight[0])
    second_weights = (query_weight[1], key_weight[1], value_weight[1], output_weight[1], up_weight[1], down_weight[1])

    def column_group(block_input):
        lifted = jnp.einsum('cxzy,cd->xzyd', block_input, lift_weight, precision=lax.Precision.HIGHEST) + lift_bias
        features = jax.nn.gelu(rms_scale(lifted, norm_gains[0])).astype(jnp.bfloat16)
        first_pass = mixer(features.reshape(first_extent, group_size * second_extent, D), 0, first_weights, norm_gains[1:3])
        second_pass = mixer(first_pass.reshape(first_extent * group_size, second_extent, D), 1, second_weights, norm_gains[3:5])
        final_norm = rms_scale(second_pass.astype(jnp.float32), norm_gains[5]).astype(jnp.bfloat16)
        coefficient = 0.05 + 0.45 * jax.nn.sigmoid(matmul(final_norm, head_weight))
        return coefficient.reshape(first_extent, group_size, second_extent, FIELDS)
    coarse_eddy = lax.map(column_group, grouped)
    coarse_eddy = jnp.transpose(coarse_eddy, (4, 1, 3, 0, 2)).reshape(FIELDS, first_extent, second_extent, third_extent)
    eddy_field = refine(refine(refine(periodic(coarse_eddy), 3), 2), 1)
    return (state_next, eddy_field)
```

```python
import functools
import math

import jax
import jax.numpy as jnp
import numpy as np
from jax import lax
from jax.experimental import pallas as pl
from jax.experimental.pallas import tpu as pltpu
from jax.sharding import PartitionSpec as P

EPSILON = 1e-06
TIME_STEP = 0.3
HALO = 5
MASKED = -1e30
F32 = jnp.float32
BF16 = jnp.bfloat16
VMEM = pl.BlockSpec(memory_space=pltpu.VMEM)


def call(body, outs, args, scratch=(), flops=0, moved=0):
    return pl.pallas_call(
        body,
        out_shape=tuple(jax.ShapeDtypeStruct(s, d) for s, d in outs),
        in_specs=[VMEM] * len(args),
        out_specs=tuple([VMEM] * len(outs)),
        scratch_shapes=list(scratch),
        cost_estimate=pl.CostEstimate(flops=flops, bytes_accessed=moved, transcendentals=0),
    )(*args)


def iota(shape, dim):
    return lax.broadcasted_iota(jnp.int32, shape, dim)


def pack_kernel(nx, ny, flow, visc, *rest):
    outs, turned = rest[:nx], rest[nx]
    fields, xl, yl, zl = flow.shape
    lanes = xl * yl
    both = 2 * fields
    for f in range(both):
        source = flow[f] if f < fields else visc[f - fields]
        turned[pl.ds(f, zl, stride=both), :] = source.reshape(lanes, zl).T
    rows = zl * both // (nx * ny)
    a, b = lax.axis_index("gx"), lax.axis_index("gy")
    for d in range(nx):
        for e in range(ny):
            chunk = lax.rem(a + d, nx) * ny + lax.rem(b + e, ny)
            start = pl.multiple_of(chunk * rows, 8)
            outs[d][e] = turned[pl.ds(start, rows), :]


def unify_kernel(nx, fields, ring, *refs):
    parts, got = refs[:nx], refs[nx]
    whole = refs[nx + 1]
    ends = refs[nx + 2 :]
    a, b = lax.axis_index("gx"), lax.axis_index("gy")
    rows, lanes = got.shape[1:]
    zc = rows // (2 * fields)
    low = iota((zc, 2 * fields, lanes), 1) < fields
    first = jnp.full((zc, 2 * fields, lanes), b) == 0
    for d in range(nx):
        mine = parts[d][0].reshape(zc, 2 * fields, lanes)
        theirs = got[d].reshape(zc, 2 * fields, lanes)
        p = jnp.where(first, mine, theirs)
        q = jnp.where(first, theirs, mine)
        where_from = lax.rem(a + nx - d, nx)
        whole[:, 0, where_from] = jnp.where(low, p, pltpu.roll(q, fields, 1))
        whole[:, 1, where_from] = jnp.where(low, pltpu.roll(p, fields, 1), q)
    for s, count in enumerate(ring):
        ends[2 * s][...] = whole[:count]
        ends[2 * s + 1][...] = whole[zc - count :]


class Shifts:
    def __init__(self, shape, yl, fields):
        self.lanes, self.yl, self.fields = shape[-1], yl, fields
        lane = iota(shape, 2)
        self.last_x = lane >= self.lanes - yl
        self.first_x = lane < yl
        inner = lax.rem(lane, yl)
        self.last_y = inner == yl - 1
        self.first_y = inner == 0

    def pairs(self, v):
        n, yl = self.lanes, self.yl
        r = pltpu.roll(v, n - yl, 2)
        xp = jnp.where(self.last_x, jnp.concatenate([r[1:], r[:1]], 0), r)
        r = pltpu.roll(v, yl, 2)
        xm = jnp.where(self.first_x, jnp.concatenate([r[-1:], r[:-1]], 0), r)
        other = pltpu.roll(v, self.fields, 1)
        yp = jnp.where(self.last_y, pltpu.roll(other, yl - 1, 2), pltpu.roll(v, n - 1, 2))
        ym = jnp.where(self.first_y, pltpu.roll(other, n - yl + 1, 2), pltpu.roll(v, 1, 2))
        return xp, xm, yp, ym


def stencil_kernel(nx, ny, fields, yl, blocks, first_state, planes, send, *refs):
    ins, refs = refs[:blocks], refs[blocks:]
    filtered, refs = refs[0], refs[1:]
    if send:
        outs, refs = refs[:nx], refs[nx:]
    whole, coef, one, two, three = refs
    position = 0
    for ref in ins:
        count = ref.shape[0]
        whole[position : position + count] = ref[...]
        position += count
    zz = position
    shape = whole.shape[2:]
    lanes = shape[-1]
    shifts = Shifts(shape, yl, fields)
    upper = iota(shape, 1) < fields

    def coefficients(z, carry):
        nu = whole[z, 1]
        for k, other in enumerate(shifts.pairs(nu)):
            coef[z, k] = 0.5 * (nu + other)
        coef[z, 4] = 0.5 * (nu + whole[z + 1, 1])
        coef[z, 5] = 0.5 * (nu + whole[z - 1, 1])
        return carry

    lax.fori_loop(1, zz - 1, coefficients, 0)

    def half_velocity(load, d):
        top = jnp.broadcast_to(load(d), shape)
        bottom = jnp.broadcast_to(load(fields + d), shape)
        return 0.5 * jnp.where(upper, top, bottom)

    def advanced(load, row, z):
        c = load(z)
        xp, xm, yp, ym = shifts.pairs(c)
        zp, zm = load(z + 1), load(z - 1)
        total = None
        for d, (p, m) in enumerate(((xp, xm), (yp, ym), (zp, zm))):
            h = half_velocity(lambda r: row(z, r), d)
            term = (coef[z, 2 * d] - h) * (p - c) + (coef[z, 2 * d + 1] + h) * (m - c)
            total = term if total is None else total + term
        return c + TIME_STEP * total

    def segment_one(z, carry):
        one[z] = advanced(
            lambda i: whole[i, 0], lambda i, r: whole[i, 0, :, r : r + 1, :], z
        )
        return carry

    def segment_two(z, carry):
        moved = advanced(lambda i: one[i], lambda i, r: one[i, :, r : r + 1, :], z)
        two[z] = 0.75 * whole[z, 0] + 0.25 * moved
        return carry

    def last_segment(z, carry):
        moved = advanced(lambda i: two[i], lambda i, r: two[i, :, r : r + 1, :], z)
        three[z] = whole[z, 0] * (1.0 / 3.0) + (2.0 / 3.0) * moved
        return carry

    lax.fori_loop(1, zz - 1, segment_one, 0)
    lax.fori_loop(2, zz - 2, segment_two, 0)
    lax.fori_loop(3, zz - 3, last_segment, 0)

    if send:
        a, b = lax.axis_index("gx"), lax.axis_index("gy")
        zc = outs[0].shape[1] // fields
        mask = iota((zc // 2, 2 * fields, lanes), 1) < fields
        first = jnp.full((zc // 2, 2 * fields, lanes), b) == 0
        for d in range(nx):
            target = lax.rem(a + d, nx)
            block = three[first_state : first_state + zc, target]
            block = block.reshape(zc // 2, 2, 2 * fields, lanes)
            even, odd = block[:, 0], block[:, 1]
            zero = jnp.where(mask, even, pltpu.roll(odd, fields, 1))
            other = jnp.where(mask, pltpu.roll(even, fields, 1), odd)
            outs[d][0] = jnp.where(first, zero, other).reshape(zc * fields, lanes)
            outs[d][1] = jnp.where(first, other, zero).reshape(zc * fields, lanes)

    for i, plane in enumerate(planes):
        z = first_state + 2 * plane
        s0, s1 = three[z], three[z + 1]
        rows = []
        for value in (s0 + s1, s0 * s0 + s1 * s1):
            value = value + pltpu.roll(value, lanes - yl, 2)
            rows.append(value + pltpu.roll(value, lanes - 1, 2))
        both = jnp.concatenate(rows, axis=1)
        height = both.shape[1]
        for part in range(3):
            rounded = both.astype(BF16)
            both = both - rounded.astype(F32)
            for k in range(shape[0]):
                filtered[
                    i, part * height : (part + 1) * height, k * lanes : (k + 1) * lanes
                ] = rounded[k]


def gelu(x):
    inner = x * (0.7978845608028654 + 0.035677408136300125 * (x * x))
    half = 0.5 * x
    return half + half * jnp.tanh(inner)


def rms_scale(v, gain):
    return v * lax.rsqrt(jnp.mean(v * v, axis=-1, keepdims=True) + EPSILON) * gain


def matmul(v, w):
    return jnp.dot(v, w, preferred_element_type=F32)


def against(v, w):
    return lax.dot_general(v, w, (((1,), (1,)), ((), ())), preferred_element_type=F32)


def mixer(section, groups, same, weights, gains):
    qkv_w, out_w, up_w, down_w = weights
    channels = section.shape[1]
    carried = section.astype(F32)
    normed = rms_scale(carried, gains[0]).astype(BF16)
    qkv = matmul(normed, qkv_w).astype(BF16)
    scale = channels ** (-0.5)
    pieces = {}
    for group in groups:
        rows = jnp.concatenate([qkv[s : s + n] for s, n in group], axis=0)
        q = rows[:, :channels]
        k = rows[:, channels : 2 * channels]
        v = rows[:, 2 * channels :]
        scores = jnp.where(same, against(q, k) * scale, MASKED)
        exponent = jnp.exp(scores - jnp.max(scores, axis=-1, keepdims=True))
        total = jnp.sum(exponent, axis=-1, keepdims=True)
        attention = (exponent * (1.0 / total)).astype(BF16)
        result = matmul(attention, v).astype(BF16)
        at = 0
        for s, n in group:
            pieces[s] = result[at : at + n]
            at += n
    attended = jnp.concatenate([pieces[s] for s in sorted(pieces)], axis=0)
    residual = carried + matmul(attended, out_w)
    again = rms_scale(residual, gains[1]).astype(BF16)
    hidden = gelu(matmul(again, up_w)).astype(BF16)
    return (residual + matmul(hidden, down_w)).astype(BF16)


def attention_kernel(nx, ny, fields, cells, step, last, earlier, *refs):
    (filtered, sel, lift_w, bias, gains, qkv_w, out_w, up_w, down_w, head), refs = (
        refs[:10],
        refs[10:],
    )
    if last:
        if earlier:
            before, refs = refs[0], refs[1:]
        spread, refs = refs[0], refs[1:]
        outs, coefficient = refs[:nx], refs[nx]
    else:
        coefficient = refs[0]
    xc, yc = cells
    channels = bias.shape[1]
    planes, height, wide = filtered.shape
    side = nx * xc * yc
    per_plane = ny * side
    span = sel.shape[0]
    cut = sel.shape[1]
    along_x = [[(p * per_plane + b * side, side)] for p in range(step) for b in range(ny)]
    together = max(1, 128 // (ny * xc * yc))
    piece = together * xc * yc
    along_y = [
        [(p * per_plane + b * side + g * piece, piece) for b in range(ny)]
        for p in range(step)
        for g in range(nx // together)
    ]
    row, column = iota((side, side), 0), iota((side, side), 1)
    same_x_line = lax.rem(row, yc) == lax.rem(column, yc)
    count = ny * piece
    row, column = iota((count, count), 0), iota((count, count), 1)
    same_y_line = lax.rem(row, piece) // yc == lax.rem(column, piece) // yc

    def some_planes(i, carry):
        block = filtered[pl.ds(i * step, step)].reshape(step * height, wide)
        found = []
        for g in range(wide // span):
            picked = matmul(block[:, g * span : (g + 1) * span], sel[...])
            third = height // 3
            found.append(
                [
                    picked[p * height : p * height + third]
                    + picked[p * height + third : p * height + 2 * third]
                    + picked[p * height + 2 * third : (p + 1) * height]
                    for p in range(step)
                ]
            )
        lifted = []
        for p in range(step):
            by_core = [[] for _ in range(ny)]
            for g in range(wide // span):
                both = lax.dot_general(
                    found[g][p],
                    lift_w[...],
                    (((0,), (0,)), ((), ())),
                    precision=lax.Precision.HIGHEST,
                    preferred_element_type=F32,
                )
                for b in range(ny):
                    by_core[b].append(both[:, b * channels : (b + 1) * channels])
            for b in range(ny):
                lifted += by_core[b]
        lifted = jnp.concatenate(lifted, axis=0) + bias[...]
        features = gelu(rms_scale(lifted, gains[0:1])).astype(BF16)
        first = mixer(
            features,
            along_x,
            same_x_line,
            (qkv_w[0], out_w[0], up_w[0], down_w[0]),
            (gains[1:2], gains[2:3]),
        )
        second = mixer(
            first,
            along_y,
            same_y_line,
            (qkv_w[1], out_w[1], up_w[1], down_w[1]),
            (gains[3:4], gains[4:5]),
        )
        final = rms_scale(second.astype(F32), gains[5:6]).astype(BF16)
        logits = against(head[0], final[:per_plane])
        for p in range(1, step):
            logits = logits + against(head[p], final[p * per_plane : (p + 1) * per_plane])
        coefficient[i] = 0.05 + 0.45 * jax.nn.sigmoid(logits)
        return carry

    lax.fori_loop(0, planes // step, some_planes, 0)

    if last:
        a, b = lax.axis_index("gx"), lax.axis_index("gy")
        every = coefficient[...].reshape(-1, per_plane)
        if earlier:
            every = jnp.concatenate([before[...].reshape(-1, per_plane), every], axis=0)
        depth = outs[0].shape[1]
        if every.shape[0] < depth:
            blank = jnp.zeros((depth - every.shape[0], per_plane), F32)
            every = jnp.concatenate([every, blank], axis=0)
        every = every.astype(BF16).astype(F32)
        width = spread.shape[1] // ny
        first = jnp.full((depth, width), b) == 0
        for d in range(nx):
            target = lax.rem(a + d, nx)
            shift = lax.rem((nx + 1 - target) * (xc * yc), side)
            near = [
                pltpu.roll(every[:, k * side : (k + 1) * side], shift, 1)[:, :cut]
                for k in range(ny)
            ]
            near = jnp.concatenate(near, axis=1).astype(BF16)
            found = matmul(near, spread[...])
            zero, other = found[:, :width], found[:, width:]
            outs[d][0] = jnp.where(first, zero, other).astype(BF16)
            outs[d][1] = jnp.where(first, other, zero).astype(BF16)


def state_kernel(nx, ny, *refs):
    parts, got, out, rows = refs[:nx], refs[nx], refs[nx + 1], refs[nx + 2]
    fields, xl, yl, zl = out.shape
    a, b = lax.axis_index("gx"), lax.axis_index("gy")
    size = got.shape[1]
    for d in range(nx):
        source = lax.rem(a + nx - d, nx)
        mine = pl.multiple_of((source * ny + b) * size, 8)
        theirs = pl.multiple_of((source * ny + lax.rem(b + 1, ny)) * size, 8)
        rows[pl.ds(mine, size), :] = parts[d][0]
        rows[pl.ds(theirs, size), :] = got[d]
    for f in range(fields):
        out[f] = rows[pl.ds(f, zl, stride=fields), :].T.reshape(xl, yl, zl)


def refine_kernel(nx, ny, *refs):
    parts, (got, along_z, across, out, rows) = refs[:nx], refs[nx:]
    fields, xl, yl, zl = out.shape
    a, b = lax.axis_index("gx"), lax.axis_index("gy")
    for d in range(nx):
        source = lax.rem(a + nx - d, nx)
        rows[source * ny + b] = parts[d][0]
        rows[source * ny + lax.rem(b + 1, ny)] = got[d]
    count, depth, width = rows.shape
    coarse = rows[...].reshape(count * depth, width)
    spread = lax.dot_general(
        coarse, along_z[...], (((0,), (0,)), ((), ())), preferred_element_type=F32
    )
    total = None
    for part in range(3):
        rounded = spread.astype(BF16)
        spread = spread - rounded.astype(F32)
        product = matmul(across[...], rounded)
        total = product if total is None else total + product
    for f in range(fields):
        out[f] = total[:, f * zl : (f + 1) * zl].reshape(xl, yl, zl)


def pick_matrix(group, xl, yl):
    xc, yc = xl // 2, yl // 2
    table = np.zeros((group, xl, yl, group, xc, yc), np.float32)
    for k in range(group):
        for x in range(xc):
            for y in range(yc):
                table[k, 2 * x, 2 * y, k, x, y] = 0.125
    return table.reshape(group * xl * yl, group * xc * yc)


def spread_matrix(ny, near, xc, yc, width):
    table = np.zeros((ny, near, xc, yc, ny, width), np.float32)
    for target in range(ny):
        for i in range(xc + 2):
            x = i - 1 + xc
            for j in range(yc + 2):
                y = (target * yc + j - 1) % (ny * yc)
                table[y // yc, x // xc, x % xc, y % yc, target, i * (yc + 2) + j] = 1.0
    return table.reshape(ny * near * xc * yc, ny * width)


def taps(fine):
    return ((fine // 2, 0.75), (fine // 2 + (1 if fine % 2 else -1), 0.25))


def across_matrix(xl, yl, width):
    yc = yl // 2
    table = np.zeros((xl, yl, width), np.float32)
    for x in range(xl):
        for y in range(yl):
            for i, u in taps(x):
                for j, v in taps(y):
                    table[x, y, (i + 1) * (yc + 2) + j + 1] += u * v
    return table.reshape(xl * yl, width)


def along_z_matrix(chunks, depth, place, fields, zc):
    table = np.zeros((chunks, depth, fields, chunks, zc), np.float32)
    for c in range(chunks):
        for z in range(zc):
            for i, u in taps(z):
                for f in range(fields):
                    table[c, place[i] + f, f, c, z] += u
    return table.reshape(chunks * depth, fields * chunks * zc)


def over_x(messages, nx):
    received = [messages[0]]
    for d in range(1, nx):
        received.append(lax.ppermute(messages[d], "gx", [(i, (i + d) % nx) for i in range(nx)]))
    return received


def over_y(received, ny):
    away = jnp.stack([piece[1] for piece in received], axis=0)
    return lax.ppermute(away, "gy", [(i, (i + 1) % ny) for i in range(ny)])


def per_device(
    nx,
    ny,
    nz,
    flow_state,
    viscosity,
    lift_weight,
    lift_bias,
    norm_gains,
    query_weight,
    key_weight,
    value_weight,
    output_weight,
    up_weight,
    down_weight,
    head_weight,
):
    fields, xl, yl, zl = flow_state.shape
    lanes = xl * yl
    chunks = nx * ny
    zc = zl // chunks
    half = zc // 2
    xc, yc = xl // 2, yl // 2
    channels = lift_bias.shape[0]
    hidden = up_weight.shape[-1]
    both = 2 * fields
    per_plane = chunks * xc * yc

    eye = jnp.eye(ny, dtype=F32)
    lift_w = lift_weight.reshape(2, 1, fields, 1, channels) * eye.reshape(1, ny, 1, ny, 1)
    lift_w = lift_w.reshape(2 * ny * fields, ny * channels)
    qkv_w = jnp.concatenate([query_weight, key_weight, value_weight], axis=-1)
    group = max(1, 512 // lanes)
    sel = jnp.asarray(pick_matrix(group, xl, yl), BF16)
    turned_head = head_weight.T

    packed = call(
        functools.partial(pack_kernel, nx, ny),
        [((ny, zc * both, lanes), F32)] * nx,
        [flow_state, viscosity],
        [pltpu.VMEM((zl * both, lanes), F32)],
        flops=1000000,
        moved=4 * zl * both * lanes,
    )
    received = over_x(packed, nx)
    got = over_y(received, ny)
    ring = []
    while sum(ring) < HALO:
        ring.append(min(zc, HALO - sum(ring)))
    block = (2, nx, ny * fields, lanes)
    unified = call(
        functools.partial(unify_kernel, nx, fields, ring),
        [((zc,) + block, F32)] + [((n,) + block, F32) for n in ring for _ in range(2)],
        [*received, got],
        flops=1000000,
        moved=8 * zl * both * lanes,
    )
    own, ends = unified[0], unified[1:]
    total = nz * chunks

    def ring_step(value, move):
        pairs = []
        for k in range(total):
            t = (k + move) % total
            pairs.append(((k % chunks) * nz + k // chunks, (t % chunks) * nz + t // chunks))
        return lax.ppermute(value, ("gx", "gy", "gz"), pairs)

    above = [ring_step(ends[2 * s], -(s + 1)) for s in range(len(ring))]
    below = [ring_step(ends[2 * s + 1], s + 1) for s in range(len(ring))]

    inner = list(range(2, half - 2))
    outer = [p for p in range(-1, half + 1) if p not in inner]

    def stencil(inputs, first_state, planes, send):
        zz = sum(v.shape[0] for v in inputs)
        size = (zz,) + block[1:]
        outs = [((len(planes), 3 * 2 * ny * fields, nx * lanes), BF16)]
        if send:
            outs += [((ny, zc * fields, lanes), F32)] * nx
        return call(
            functools.partial(
                stencil_kernel, nx, ny, fields, yl, len(inputs), first_state, planes, send
            ),
            outs,
            inputs,
            [
                pltpu.VMEM((zz,) + block, F32),
                pltpu.VMEM((zz, 6) + block[1:], F32),
                pltpu.VMEM(size, F32),
                pltpu.VMEM(size, F32),
                pltpu.VMEM(size, F32),
            ],
            flops=300000000,
            moved=8 * zz * nx * 8 * lanes,
        )

    def pairing(planes):
        return 2 if len(planes) % 2 == 0 else 1

    def heads(step):
        out = jnp.zeros((step, 8, channels), BF16)
        for p in range(step):
            out = out.at[p, p * fields : (p + 1) * fields].set(turned_head)
        return out

    def attention(filtered, planes, more, outs, last):
        step = pairing(planes)
        args = [
            filtered,
            sel,
            lift_w,
            lift_bias.reshape(1, channels),
            norm_gains,
            qkv_w,
            output_weight,
            up_weight,
            down_weight,
            heads(step),
        ] + more
        size = (len(planes) // step, 8, per_plane)
        work = len(planes) * per_plane * channels * (8 * channels + 4 * hidden) * 2
        return call(
            functools.partial(
                attention_kernel, nx, ny, fields, (xc, yc), step, last, len(more) > 1
            ),
            outs if last else [(size, F32)],
            args,
            [pltpu.VMEM(size, F32)] if last else [],
            flops=3 * work,
            moved=1000000,
        )

    place = {}
    depth = 0
    for planes in (inner, outer):
        step = pairing(planes)
        for i, p in enumerate(planes):
            place[p] = depth + (i // step) * 8 + (i % step) * fields
        depth += len(planes) // step * 8
    depth = -(-depth // 16) * 16

    more = []
    if inner:
        (filtered,) = stencil([own], 0, inner, False)
        more = list(attention(filtered, inner, [], None, False))

    ordered = below[::-1] + [own] + above
    second = stencil(ordered, HALO, outer, True)
    filtered, state_messages = second[0], list(second[1:])
    state_received = over_x(state_messages, nx)

    width = -(-(xc + 2) * (yc + 2) // 128) * 128
    near = 128 // (xc * yc)
    spread = jnp.asarray(spread_matrix(ny, near, xc, yc, width), BF16)
    messages = attention(
        filtered, outer, more + [spread], [((ny, depth, width), BF16)] * nx, True
    )
    coarse_received = over_x(list(messages), nx)
    state_got = over_y(state_received, ny)
    (state_next,) = call(
        functools.partial(state_kernel, nx, ny),
        [(flow_state.shape, F32)],
        [*state_received, state_got],
        [pltpu.VMEM((zl * fields, lanes), F32)],
        flops=1000000,
        moved=8 * zl * fields * lanes,
    )
    coarse_got = over_y(coarse_received, ny)
    along_z = jnp.asarray(along_z_matrix(chunks, depth, place, fields, zc), BF16)
    across = jnp.asarray(across_matrix(xl, yl, width), BF16)
    (eddy_field,) = call(
        functools.partial(refine_kernel, nx, ny),
        [(flow_state.shape, F32)],
        [*coarse_received, coarse_got, along_z, across],
        [pltpu.VMEM((chunks, depth, width), BF16)],
        flops=1000000,
        moved=8 * zl * fields * lanes,
    )
    return (state_next, eddy_field)


def solution(mesh):
    sizes = [mesh.shape[name] for name in ("gx", "gy", "gz")]
    return jax.shard_map(
        functools.partial(per_device, *sizes),
        mesh=mesh,
        in_specs=(
            P(None, "gx", "gy", "gz"),
            P(None, "gx", "gy", "gz"),
            P(),
            P(),
            P(),
            P(),
            P(),
            P(),
            P(),
            P(),
            P(),
            P(),
        ),
        out_specs=(P(None, "gx", "gy", "gz"), P(None, "gx", "gy", "gz")),
        check_vma=False,
    )
```

```python
import functools

import jax
import jax.numpy as jnp
import numpy as np
from jax import lax
from jax.experimental import pallas as pl
from jax.experimental.pallas import tpu as pltpu
from jax.sharding import PartitionSpec as P

EPSILON = 1e-06
TIME_STEP = 0.3
HALO = 5
MASKED = -1e30
F32 = jnp.float32
BF16 = jnp.bfloat16
VMEM = pl.BlockSpec(memory_space=pltpu.VMEM)


def call(body, outs, args, scratch=(), flops=0, moved=0, room=16):
    return pl.pallas_call(
        body,
        out_shape=tuple(jax.ShapeDtypeStruct(s, d) for s, d in outs),
        in_specs=[VMEM] * len(args),
        out_specs=tuple([VMEM] * len(outs)),
        scratch_shapes=list(scratch),
        cost_estimate=pl.CostEstimate(flops=flops, bytes_accessed=moved, transcendentals=0),
        compiler_params=pltpu.CompilerParams(vmem_limit_bytes=min(room, 60) * 1048576),
    )(*args)


def iota(shape, dim):
    return lax.broadcasted_iota(jnp.int32, shape, dim)


def pack_kernel(nx, ny, flow, visc, *rest):
    outs, turned = rest[:nx], rest[nx]
    fields, xl, yl, zl = flow.shape
    lanes = xl * yl
    both = 2 * fields
    for f in range(both):
        source = flow[f] if f < fields else visc[f - fields]
        turned[pl.ds(f, zl, stride=both), :] = source.reshape(lanes, zl).T
    rows = zl * both // (nx * ny)
    a, b = lax.axis_index("gx"), lax.axis_index("gy")
    for d in range(nx):
        for e in range(ny):
            chunk = lax.rem(a + d, nx) * ny + lax.rem(b + e, ny)
            start = pl.multiple_of(chunk * rows, 8)
            outs[d][e] = turned[pl.ds(start, rows), :]


def unify_kernel(nx, fields, ring, *refs):
    parts, got = refs[:nx], refs[nx]
    whole = refs[nx + 1]
    ends = refs[nx + 2 :]
    a, b = lax.axis_index("gx"), lax.axis_index("gy")
    rows, lanes = got.shape[1:]
    zc = rows // (2 * fields)
    low = iota((zc, 2 * fields, lanes), 1) < fields
    first = jnp.full((zc, 2 * fields, lanes), b) == 0
    for d in range(nx):
        mine = parts[d][0].reshape(zc, 2 * fields, lanes)
        theirs = got[d].reshape(zc, 2 * fields, lanes)
        p = jnp.where(first, mine, theirs)
        q = jnp.where(first, theirs, mine)
        where_from = lax.rem(a + nx - d, nx)
        whole[:, 0, where_from] = jnp.where(low, p, pltpu.roll(q, fields, 1))
        whole[:, 1, where_from] = jnp.where(low, pltpu.roll(p, fields, 1), q)
    for s, count in enumerate(ring):
        ends[2 * s][...] = whole[:count]
        ends[2 * s + 1][...] = whole[zc - count :]


class Shifts:
    def __init__(self, shape, yl, fields):
        self.lanes, self.yl, self.fields = shape[-1], yl, fields
        lane = iota(shape, 2)
        self.last_x = lane >= self.lanes - yl
        self.first_x = lane < yl
        inner = lax.rem(lane, yl)
        self.last_y = inner == yl - 1
        self.first_y = inner == 0

    def pairs(self, v):
        n, yl = self.lanes, self.yl
        r = pltpu.roll(v, n - yl, 2)
        xp = jnp.where(self.last_x, jnp.concatenate([r[1:], r[:1]], 0), r)
        r = pltpu.roll(v, yl, 2)
        xm = jnp.where(self.first_x, jnp.concatenate([r[-1:], r[:-1]], 0), r)
        other = pltpu.roll(v, self.fields, 1)
        yp = jnp.where(self.last_y, pltpu.roll(other, yl - 1, 2), pltpu.roll(v, n - 1, 2))
        ym = jnp.where(self.first_y, pltpu.roll(other, n - yl + 1, 2), pltpu.roll(v, 1, 2))
        return xp, xm, yp, ym


def stencil_kernel(nx, ny, fields, yl, blocks, first_state, planes, inner, outer, *refs):
    ins, refs = refs[:blocks], refs[blocks:]
    kept = ()
    if outer and inner:
        kept, refs = refs[:3], refs[3:]
    filtered, refs = refs[0], refs[1:]
    if outer:
        outs, refs = refs[:nx], refs[nx:]
        whole, coef, one, two, three = refs
    else:
        one, two, three, whole, coef = refs
    position = 0
    for ref in ins:
        count = ref.shape[0]
        whole[position : position + count] = ref[...]
        position += count
    zz = position
    zc = zz - 2 * first_state
    shape = whole.shape[2:]
    lanes = shape[-1]
    shifts = Shifts(shape, yl, fields)
    upper = iota(shape, 1) < fields

    def planes_of(margin):
        due = range(margin, zz - margin)
        if kept:
            own = range(first_state + margin, first_state + zc - margin)
            due = [z for z in due if z not in own]
        due = sorted(due, key=lambda z: min(z, zz - 1 - z))
        return due

    for z in sorted({z for margin in (1, 2, 3) for z in planes_of(margin)}):
        nu = whole[z, 1]
        total = None
        for k, other in enumerate((*shifts.pairs(nu), whole[z + 1, 1], whole[z - 1, 1])):
            face = nu + other
            coef[z, k] = face
            total = face if total is None else total + face
        coef[z, 6] = 1.0 - (0.5 * TIME_STEP) * total

    def advanced(load, row, z):
        c = load(z)
        xp, xm, yp, ym = shifts.pairs(c)
        total = None
        for d, (p, m) in enumerate(((xp, xm), (yp, ym), (load(z + 1), load(z - 1)))):
            top = jnp.broadcast_to(row(z, d), shape)
            velocity = jnp.where(upper, top, jnp.broadcast_to(row(z, fields + d), shape))
            term = (coef[z, 2 * d] - velocity) * p + (coef[z, 2 * d + 1] + velocity) * m
            total = term if total is None else total + term
        return c * coef[z, 6] + (0.5 * TIME_STEP) * total

    for z in planes_of(1):
        one[z] = advanced(lambda i: whole[i, 0], lambda i, r: whole[i, 0, :, r : r + 1, :], z)
    if kept:
        for z in (1, 2, zc - 3, zc - 2):
            one[first_state + z] = kept[0][z]
        for z in (2, 3, zc - 4, zc - 3):
            two[first_state + z] = kept[1][z]
        three[first_state + 3 : first_state + zc - 3] = kept[2][3 : zc - 3]
    for z in planes_of(2):
        moved = advanced(lambda i: one[i], lambda i, r: one[i, :, r : r + 1, :], z)
        two[z] = 0.75 * whole[z, 0] + 0.25 * moved
    for z in planes_of(3):
        moved = advanced(lambda i: two[i], lambda i, r: two[i, :, r : r + 1, :], z)
        three[z] = whole[z, 0] * (1.0 / 3.0) + (2.0 / 3.0) * moved

    if outer:
        a, b = lax.axis_index("gx"), lax.axis_index("gy")
        mask = iota((zc // 2, 2 * fields, lanes), 1) < fields
        first = jnp.full((zc // 2, 2 * fields, lanes), b) == 0
        for d in range(nx):
            target = lax.rem(a + d, nx)
            block = three[first_state : first_state + zc, target]
            block = block.reshape(zc // 2, 2, 2 * fields, lanes)
            even, odd = block[:, 0], block[:, 1]
            zero = jnp.where(mask, even, pltpu.roll(odd, fields, 1))
            other = jnp.where(mask, pltpu.roll(even, fields, 1), odd)
            outs[d][0] = jnp.where(first, zero, other).reshape(zc * fields, lanes)
            outs[d][1] = jnp.where(first, other, zero).reshape(zc * fields, lanes)

    for i, plane in enumerate(planes):
        z = first_state + 2 * plane
        s0, s1 = three[z], three[z + 1]
        rows = []
        for value in (s0 + s1, s0 * s0 + s1 * s1):
            value = value + pltpu.roll(value, lanes - yl, 2)
            rows.append(value + pltpu.roll(value, lanes - 1, 2))
        both = jnp.concatenate(rows, axis=1)
        height = both.shape[1]
        for part in range(3):
            rounded = both.astype(BF16)
            both = both - rounded.astype(F32)
            for k in range(shape[0]):
                filtered[
                    i, part * height : (part + 1) * height, k * lanes : (k + 1) * lanes
                ] = rounded[k]


def twice_gelu(x):
    inner = x * (0.7978845608028654 + 0.035677408136300125 * (x * x))
    return x + x * jnp.tanh(inner)


def rms_scale(v, gain):
    total = jnp.sum(v * v, axis=-1, keepdims=True)
    return v * lax.rsqrt(total + EPSILON * v.shape[-1]) * gain


def matmul(v, w):
    return jnp.dot(v, w, preferred_element_type=F32)


def against(v, w):
    return lax.dot_general(v, w, (((1,), (1,)), ((), ())), preferred_element_type=F32)


def attend(section, groups, same, weights, gain):
    qkv_w, out_w = weights
    channels = section.shape[1]
    carried = section.astype(F32)
    normed = rms_scale(carried, gain).astype(BF16)
    yield
    qkv = matmul(normed, qkv_w).astype(BF16)
    yield
    scale = channels ** (-0.5) * 1.4426950408889634
    values, scores = [], []
    for group in groups:
        rows = jnp.concatenate([qkv[s : s + n] for s, n in group], axis=0)
        q, k = rows[:, :channels], rows[:, channels : 2 * channels]
        values.append(rows[:, 2 * channels :])
        scores.append(jnp.where(same, against(q, k), MASKED))
        yield
    weighted = []
    for score in scores:
        exponent = jnp.exp2((score - jnp.max(score, axis=-1, keepdims=True)) * scale)
        weighted.append(exponent.astype(BF16))
        yield
    pieces = {}
    for group, exponent, v in zip(groups, weighted, values):
        summed = matmul(exponent, jnp.concatenate([v, jnp.ones_like(v)], axis=1))
        result = (summed[:, :channels] * (1.0 / summed[:, channels:])).astype(BF16)
        at = 0
        for s, n in group:
            pieces[s] = result[at : at + n]
            at += n
        yield
    attended = jnp.concatenate([pieces[s] for s in sorted(pieces)], axis=0)
    return carried + matmul(attended, out_w)


def feed(residual, weights, gain):
    up_w, down_w = weights
    again = rms_scale(residual, gain).astype(BF16)
    yield
    rows, hidden = residual.shape[0], up_w.shape[1]
    wide, tall = min(256, hidden), min(64, rows)
    total = None
    for h in range(0, hidden, wide):
        up = matmul(again, up_w[:, h : h + wide])
        pieces = []
        for r in range(0, rows, tall):
            pieces.append(twice_gelu(up[r : r + tall]).astype(BF16))
            yield
        down = matmul(jnp.concatenate(pieces, axis=0), down_w[h : h + wide])
        total = down if total is None else total + down
        yield
    return (residual + 0.5 * total).astype(BF16)


def together(tasks):
    results = [None] * len(tasks)
    alive = dict(enumerate(tasks))
    while alive:
        for i in list(alive):
            try:
                next(alive[i])
            except StopIteration as stop:
                results[i] = stop.value
                del alive[i]
    return results


def attention_kernel(nx, ny, fields, cells, step, last, earlier, *refs):
    (filtered, sel, lift_w, bias, gains, qkv_w, out_w, up_w, down_w, head), refs = (
        refs[:10],
        refs[10:],
    )
    if last:
        if earlier:
            before, refs = refs[0], refs[1:]
        spread, refs = refs[0], refs[1:]
        outs, refs = refs[:nx], refs[nx:]
    coefficient = refs[0]
    xc, yc = cells
    channels = bias.shape[1]
    planes, height, wide = filtered.shape
    side = nx * xc * yc
    per_plane = ny * side
    cut, span = sel.shape
    along_x = [[(b * side, side)] for b in range(ny)]
    count = max(1, 128 // (ny * xc * yc))
    piece = count * xc * yc
    along_y = [
        [(b * side + g * piece, piece) for b in range(ny)] for g in range(nx // count)
    ]
    row, column = iota((side, side), 0), iota((side, side), 1)
    same_x_line = lax.rem(row, yc) == lax.rem(column, yc)
    count = ny * piece
    row, column = iota((count, count), 0), iota((count, count), 1)
    same_y_line = lax.rem(row, piece) // yc == lax.rem(column, piece) // yc
    gain = [gains[i : i + 1] * channels**0.5 for i in range(6)]

    def lift_and_first(block):
        by_core = [[] for _ in range(ny)]
        for g in range(wide // span):
            parts = block[:, g * span : (g + 1) * span]
            picked = against(sel[...], jnp.concatenate([parts] * 3, axis=0)).astype(BF16)
            yield
            both = matmul(picked, lift_w[...])
            for b in range(ny):
                by_core[b].append(both[:, b * channels : (b + 1) * channels])
        yield
        features = []
        for rows in sum(by_core, []):
            lifted = rows + bias[...]
            features.append((0.5 * twice_gelu(rms_scale(lifted, gain[0]))).astype(BF16))
            yield
        features = jnp.concatenate(features, axis=0)
        weights = qkv_w[0], out_w[0]
        return (yield from attend(features, along_x, same_x_line, weights, gain[1]))

    def first_feed(residual):
        return feed(residual, (up_w[0], down_w[0]), gain[2])

    def second(value):
        return attend(value, along_y, same_y_line, (qkv_w[1], out_w[1]), gain[3])

    def second_feed_and_head(residual, turned, plus):
        value = yield from feed(residual, (up_w[1], down_w[1]), gain[4])
        final = rms_scale(value.astype(F32), gain[5]).astype(BF16)
        yield
        logits = against(turned, final)
        return logits if plus is None else logits + plus

    def coefficient_of(logits):
        return 0.05 + 0.45 * jax.nn.sigmoid(logits)

    def chain(plane, turned):
        value = yield from lift_and_first(plane)
        value = yield from first_feed(value)
        value = yield from second(value)
        return (yield from second_feed_and_head(value, turned, None))

    def some_planes(i, carry):
        tasks = [chain(filtered[i * width + p], head[p % step]) for p in range(width)]
        found = together(tasks)
        for p in range(0, width, step):
            row = i * (width // step) + p // step
            coefficient[row] = coefficient_of(sum(found[p + 1 : p + step], found[p]))
        return carry

    width = planes if planes * per_plane <= 2048 else step
    lax.fori_loop(0, planes // width, some_planes, 0)

    if last:
        a, b = lax.axis_index("gx"), lax.axis_index("gy")
        every = coefficient[...].reshape(-1, per_plane)
        if earlier:
            every = jnp.concatenate([before[...].reshape(-1, per_plane), every], axis=0)
        depth = outs[0].shape[1]
        if every.shape[0] < depth:
            blank = jnp.zeros((depth - every.shape[0], per_plane), F32)
            every = jnp.concatenate([every, blank], axis=0)
        every = every.astype(BF16).astype(F32)
        width = spread.shape[1] // ny
        first = jnp.full((depth, width), b) == 0
        for d in range(nx):
            target = lax.rem(a + d, nx)
            shift = lax.rem((nx + 1 - target) * (xc * yc), side)
            near = [
                pltpu.roll(every[:, k * side : (k + 1) * side], shift, 1)[:, :cut]
                for k in range(ny)
            ]
            near = jnp.concatenate(near, axis=1).astype(BF16)
            found = matmul(near, spread[...])
            zero, other = found[:, :width], found[:, width:]
            outs[d][0] = jnp.where(first, zero, other).astype(BF16)
            outs[d][1] = jnp.where(first, other, zero).astype(BF16)


def state_kernel(nx, ny, *refs):
    parts, got, out, rows = refs[:nx], refs[nx], refs[nx + 1], refs[nx + 2]
    fields, xl, yl, zl = out.shape
    a, b = lax.axis_index("gx"), lax.axis_index("gy")
    size = got.shape[1]
    for d in range(nx):
        source = lax.rem(a + nx - d, nx)
        mine = pl.multiple_of((source * ny + b) * size, 8)
        theirs = pl.multiple_of((source * ny + lax.rem(b + 1, ny)) * size, 8)
        rows[pl.ds(mine, size), :] = parts[d][0]
        rows[pl.ds(theirs, size), :] = got[d]
    for f in range(fields):
        out[f] = rows[pl.ds(f, zl, stride=fields), :].T.reshape(xl, yl, zl)


def refine_kernel(nx, ny, *refs):
    parts, (got, along_z, across, out, rows) = refs[:nx], refs[nx:]
    fields, xl, yl, zl = out.shape
    a, b = lax.axis_index("gx"), lax.axis_index("gy")
    for d in range(nx):
        source = lax.rem(a + nx - d, nx)
        rows[source * ny + b] = parts[d][0]
        rows[source * ny + lax.rem(b + 1, ny)] = got[d]
    count, depth, width = rows.shape
    coarse = rows[...].reshape(count * depth, width)
    spread = lax.dot_general(
        coarse, along_z[...], (((0,), (0,)), ((), ())), preferred_element_type=F32
    )
    total = None
    for part in range(3):
        rounded = spread.astype(BF16)
        spread = spread - rounded.astype(F32)
        product = matmul(across[...], rounded)
        total = product if total is None else total + product
    for f in range(fields):
        out[f] = total[:, f * zl : (f + 1) * zl].reshape(xl, yl, zl)


def pick_matrix(group, xl, yl):
    xc, yc = xl // 2, yl // 2
    table = np.zeros((group, xl, yl, group, xc, yc), np.float32)
    for k in range(group):
        for x in range(xc):
            for y in range(yc):
                table[k, 2 * x, 2 * y, k, x, y] = 0.125
    return table.reshape(group * xl * yl, group * xc * yc)


def spread_matrix(ny, near, xc, yc, width):
    table = np.zeros((ny, near, xc, yc, ny, width), np.float32)
    for target in range(ny):
        for i in range(xc + 2):
            x = i - 1 + xc
            for j in range(yc + 2):
                y = (target * yc + j - 1) % (ny * yc)
                table[y // yc, x // xc, x % xc, y % yc, target, i * (yc + 2) + j] = 1.0
    return table.reshape(ny * near * xc * yc, ny * width)


def taps(fine):
    return ((fine // 2, 0.75), (fine // 2 + (1 if fine % 2 else -1), 0.25))


def across_matrix(xl, yl, width):
    yc = yl // 2
    table = np.zeros((xl, yl, width), np.float32)
    for x in range(xl):
        for y in range(yl):
            for i, u in taps(x):
                for j, v in taps(y):
                    table[x, y, (i + 1) * (yc + 2) + j + 1] += u * v
    return table.reshape(xl * yl, width)


def along_z_matrix(chunks, depth, place, fields, zc):
    table = np.zeros((chunks, depth, fields, chunks, zc), np.float32)
    for c in range(chunks):
        for z in range(zc):
            for i, u in taps(z):
                for f in range(fields):
                    table[c, place[i] + f, f, c, z] += u
    return table.reshape(chunks * depth, fields * chunks * zc)


def over_x(messages, nx):
    received = [messages[0]]
    for d in range(1, nx):
        received.append(lax.ppermute(messages[d], "gx", [(i, (i + d) % nx) for i in range(nx)]))
    return received


def over_y(received, ny):
    away = jnp.stack([piece[1] for piece in received], axis=0)
    return lax.ppermute(away, "gy", [(i, (i + 1) % ny) for i in range(ny)])


def per_device(
    nx,
    ny,
    nz,
    flow_state,
    viscosity,
    lift_weight,
    lift_bias,
    norm_gains,
    query_weight,
    key_weight,
    value_weight,
    output_weight,
    up_weight,
    down_weight,
    head_weight,
):
    fields, xl, yl, zl = flow_state.shape
    lanes = xl * yl
    chunks = nx * ny
    zc = zl // chunks
    half = zc // 2
    xc, yc = xl // 2, yl // 2
    channels = lift_bias.shape[0]
    hidden = up_weight.shape[-1]
    both = 2 * fields
    per_plane = chunks * xc * yc

    eye = jnp.eye(ny, dtype=F32)
    lift_w = lift_weight.reshape(2, 1, fields, 1, channels) * eye.reshape(1, ny, 1, ny, 1)
    rest = lift_w.reshape(2 * ny * fields, ny * channels)
    stacked = []
    for _ in range(3):
        rounded = lax.reduce_precision(rest, 8, 7)
        rest = rest - rounded
        stacked += [rounded] * 3
    lift_w = jnp.concatenate(stacked, axis=0).astype(BF16)
    qkv_w = jnp.concatenate([query_weight, key_weight, value_weight], axis=-1)
    group = max(1, 512 // lanes)
    sel = jnp.asarray(pick_matrix(group, xl, yl).T, BF16)
    turned_head = head_weight.T

    packed = call(
        functools.partial(pack_kernel, nx, ny),
        [((ny, zc * both, lanes), F32)] * nx,
        [flow_state, viscosity],
        [pltpu.VMEM((zl * both, lanes), F32)],
        flops=1000000,
        moved=4 * zl * both * lanes,
    )
    received = over_x(packed, nx)
    got = over_y(received, ny)
    ring = []
    while sum(ring) < HALO:
        ring.append(min(zc, HALO - sum(ring)))
    block = (2, nx, ny * fields, lanes)
    unified = call(
        functools.partial(unify_kernel, nx, fields, ring),
        [((zc,) + block, F32)] + [((n,) + block, F32) for n in ring for _ in range(2)],
        [*received, got],
        flops=1000000,
        moved=8 * zl * both * lanes,
    )
    own, ends = unified[0], unified[1:]
    total = nz * chunks

    def ring_step(value, move):
        pairs = []
        for k in range(total):
            t = (k + move) % total
            pairs.append(((k % chunks) * nz + k // chunks, (t % chunks) * nz + t // chunks))
        return lax.ppermute(value, ("gx", "gy", "gz"), pairs)

    above = [ring_step(ends[2 * s], -(s + 1)) for s in range(len(ring))]
    below = [ring_step(ends[2 * s + 1], s + 1) for s in range(len(ring))]

    inner = list(range(2, half - 2))
    outer = [p for p in range(-1, half + 1) if p not in inner]

    def stencil(inputs, first_state, planes, kept, last):
        zz = sum(v.shape[0] for v in inputs)
        size = ((zz,) + block[1:], F32)
        outs = [((len(planes), 3 * 2 * ny * fields, nx * lanes), BF16)]
        outs += [((ny, zc * fields, lanes), F32)] * nx if last else [size] * 3
        return call(
            functools.partial(
                stencil_kernel,
                nx,
                ny,
                fields,
                yl,
                len(inputs),
                first_state,
                planes,
                bool(kept) or not last,
                last,
            ),
            outs,
            [*inputs, *kept],
            [pltpu.VMEM((zz,) + block, F32), pltpu.VMEM((zz, 7) + block[1:], F32)]
            + ([pltpu.VMEM(*size)] * 3 if last else []),
            flops=300000000,
            moved=8 * zz * nx * 8 * lanes,
            room=16 * (nx // 4) ** 2,
        )

    def pairing(planes):
        return 2 if len(planes) % 2 == 0 else 1

    def heads(step):
        out = jnp.zeros((step, 8, channels), BF16)
        for p in range(step):
            out = out.at[p, p * fields : (p + 1) * fields].set(turned_head)
        return out

    def attention(filtered, planes, more, outs, last):
        step = pairing(planes)
        args = [
            filtered,
            sel,
            lift_w,
            lift_bias.reshape(1, channels),
            norm_gains,
            qkv_w,
            output_weight,
            up_weight,
            down_weight,
            heads(step),
        ] + more
        size = (len(planes) // step, 8, per_plane)
        work = len(planes) * per_plane * channels * (8 * channels + 4 * hidden) * 2
        return call(
            functools.partial(
                attention_kernel, nx, ny, fields, (xc, yc), step, last, len(more) > 1
            ),
            outs if last else [(size, F32)],
            args,
            ([pltpu.VMEM(size, F32)] if last else []),
            flops=3 * work,
            moved=1000000,
            room=16 * (nx // 4) ** 2,
        )

    place = {}
    depth = 0
    for planes in (inner, outer):
        step = pairing(planes)
        for i, p in enumerate(planes):
            place[p] = depth + (i // step) * 8 + (i % step) * fields
        depth += len(planes) // step * 8
    depth = -(-depth // 16) * 16

    more, kept = [], []
    if inner:
        filtered, *kept = stencil([own], 0, inner, [], False)
        more = list(attention(filtered, inner, [], None, False))

    ordered = below[::-1] + [own] + above
    second = stencil(ordered, HALO, outer, kept, True)
    filtered, state_messages = second[0], list(second[1:])
    state_received = over_x(state_messages, nx)

    width = -(-(xc + 2) * (yc + 2) // 128) * 128
    near = 128 // (xc * yc)
    spread = jnp.asarray(spread_matrix(ny, near, xc, yc, width), BF16)
    messages = attention(
        filtered, outer, more + [spread], [((ny, depth, width), BF16)] * nx, True
    )
    coarse_received = over_x(list(messages), nx)
    state_got = over_y(state_received, ny)
    (state_next,) = call(
        functools.partial(state_kernel, nx, ny),
        [(flow_state.shape, F32)],
        [*state_received, state_got],
        [pltpu.VMEM((zl * fields, lanes), F32)],
        flops=1000000,
        moved=8 * zl * fields * lanes,
    )
    coarse_got = over_y(coarse_received, ny)
    along_z = jnp.asarray(along_z_matrix(chunks, depth, place, fields, zc), BF16)
    across = jnp.asarray(across_matrix(xl, yl, width), BF16)
    (eddy_field,) = call(
        functools.partial(refine_kernel, nx, ny),
        [(flow_state.shape, F32)],
        [*coarse_received, coarse_got, along_z, across],
        [pltpu.VMEM((chunks, depth, width), BF16)],
        flops=1000000,
        moved=8 * zl * fields * lanes,
    )
    return (state_next, eddy_field)


def solution(mesh):
    sizes = [mesh.shape[name] for name in ("gx", "gy", "gz")]
    return jax.shard_map(
        functools.partial(per_device, *sizes),
        mesh=mesh,
        in_specs=(
            P(None, "gx", "gy", "gz"),
            P(None, "gx", "gy", "gz"),
            P(),
            P(),
            P(),
            P(),
            P(),
            P(),
            P(),
            P(),
            P(),
            P(),
        ),
        out_specs=(P(None, "gx", "gy", "gz"), P(None, "gx", "gy", "gz")),
        check_vma=False,
    )
```

```python
import functools
import math

import jax
import jax.numpy as jnp
import numpy as np
from jax import lax
from jax.experimental import pallas as pl
from jax.experimental.pallas import tpu as pltpu
from jax.sharding import PartitionSpec as P

EPSILON = 1e-06
TIME_STEP = 0.3
HALO = 5
MASKED = -1e30
F32 = jnp.float32
BF16 = jnp.bfloat16
VMEM = pl.BlockSpec(memory_space=pltpu.VMEM)
HBM = pl.BlockSpec(memory_space=pltpu.HBM)


def call(body, outs, args, scratch=(), flops=0, moved=0, room=16, where=(VMEM, VMEM)):
    return pl.pallas_call(
        body,
        out_shape=tuple(jax.ShapeDtypeStruct(s, d) for s, d in outs),
        in_specs=[where[0]] * len(args),
        out_specs=tuple([where[1]] * len(outs)),
        scratch_shapes=list(scratch),
        cost_estimate=pl.CostEstimate(flops=flops, bytes_accessed=moved, transcendentals=0),
        compiler_params=pltpu.CompilerParams(vmem_limit_bytes=int(min(room, 63.93) * 1048576)),
    )(*args)


def iota(shape, dim):
    return lax.broadcasted_iota(jnp.int32, shape, dim)


def halves(v):
    high = v.astype(BF16)
    return high, (v - high.astype(F32)).astype(BF16)


def pack_kernel(nx, ny, flow, visc, *rest):
    outs, (turned, blocks, sems) = rest[:nx], rest[nx:]
    fields, xl, yl, zl = flow.shape
    lanes = xl * yl
    both = 2 * fields
    copies = []
    for f in range(both):
        source = flow.at[f] if f < fields else visc.at[f - fields]
        copies.append(pltpu.make_async_copy(source, blocks.at[f], sems.at[f]))
        copies[f].start()
    for f in range(both):
        copies[f].wait()
        kind, row = divmod(f, fields)
        turned[kind, pl.ds(row, zl, stride=fields), :] = blocks[f].reshape(lanes, zl).T
    rows = zl * fields // (nx * ny)
    a, b = lax.axis_index("gx"), lax.axis_index("gy")
    for d in range(nx):
        for e in range(ny):
            chunk = lax.rem(a + d, nx) * ny + lax.rem(b + e, ny)
            start = pl.multiple_of(chunk * rows, 8)
            high, low = halves(turned[0, pl.ds(start, rows), :])
            outs[d][e, 0] = high
            outs[d][e, 1] = low
            outs[d][e, 2] = turned[1, pl.ds(start, rows), :].astype(BF16)


def small_kernel(ny, fields, lift, bias, gains, head, small, lift_w, head_w):
    channels = gains.shape[1]
    small[:6] = gains[...] * channels**0.5
    small[6:7] = bias[...]
    small[7:8] = bias[...]
    rest = lift[...]
    rows = rest.shape[0]
    upper = lax.rem(iota((rows, channels), 0), 2 * fields) < fields
    for part in range(3):
        rounded = rest.astype(BF16)
        rest = rest - rounded.astype(F32)
        exact = rounded.astype(F32)
        swapped = pltpu.roll(exact, fields, 0)
        for b in range(ny):
            first = exact if b == 0 else swapped
            second = swapped if b == 0 else exact
            keep = upper if b == 0 else jnp.logical_not(upper)
            both = jnp.concatenate(
                [jnp.where(keep, first, 0.0), jnp.where(keep, second, 0.0)], axis=0
            ).astype(BF16)
            for again in range(3):
                at = (part * 3 + again) * 2 * rows
                lift_w[at : at + 2 * rows, b * channels : (b + 1) * channels] = both
    turned = head[...].astype(F32).T
    turned = jnp.concatenate([turned, jnp.zeros_like(turned)], axis=0)
    head_w[0] = turned.astype(BF16)
    head_w[1] = pltpu.roll(turned, fields, 0).astype(BF16)


def sort_kernel(nx, *refs):
    parts, (mine, away) = refs[:nx], refs[-2:]
    for d in range(nx):
        mine[d] = parts[d][0]
        away[d] = parts[d][1]


def unify_kernel(nx, fields, ring, mine, got, whole, *ends):
    a, b = lax.axis_index("gx"), lax.axis_index("gy")
    rows, lanes = got.shape[2:]
    zc = rows // fields
    shape = zc // 2, 2 * fields, lanes
    low = iota(shape, 1) < fields
    first = jnp.full(shape, b) == 0
    for d in range(nx):
        where_from = lax.rem(a + nx - d, nx)
        near = mine[d].astype(F32)
        far = got[d].astype(F32)
        for kind in range(2):
            m = (near[2] if kind else near[0] + near[1]).reshape(shape)
            t = (far[2] if kind else far[0] + far[1]).reshape(shape)
            p = jnp.where(first, m, t)
            q = jnp.where(first, t, m)
            even = jnp.where(low, p, pltpu.roll(q, fields, 1))
            odd = jnp.where(low, pltpu.roll(p, fields, 1), q)
            for z in range(zc // 2):
                whole[2 * z, kind, where_from] = even[z]
                whole[2 * z + 1, kind, where_from] = odd[z]
    for s, count in enumerate(ring):
        ends[2 * s][...] = whole[:count]
        ends[2 * s + 1][...] = whole[zc - count :]


class Shifts:
    def __init__(self, shape, yl, fields):
        self.lanes, self.yl, self.fields = shape[-1], yl, fields
        lane = iota(shape, 2)
        self.last_x = lane >= self.lanes - yl
        self.first_x = lane < yl
        inner = lax.rem(lane, yl)
        self.last_y = inner == yl - 1
        self.first_y = inner == 0

    def pairs(self, v):
        n, yl = self.lanes, self.yl
        r = pltpu.roll(v, n - yl, 2)
        xp = jnp.where(self.last_x, jnp.concatenate([r[1:], r[:1]], 0), r)
        r = pltpu.roll(v, yl, 2)
        xm = jnp.where(self.first_x, jnp.concatenate([r[-1:], r[:-1]], 0), r)
        other = pltpu.roll(v, self.fields, 1)
        yp = jnp.where(self.last_y, pltpu.roll(other, yl - 1, 2), pltpu.roll(v, n - 1, 2))
        ym = jnp.where(self.first_y, pltpu.roll(other, n - yl + 1, 2), pltpu.roll(v, 1, 2))
        return xp, xm, yp, ym


def stencil_kernel(nx, ny, fields, yl, blocks, first_state, planes, inner, outer, *refs):
    ins, refs = refs[:blocks], refs[blocks:]
    kept = ()
    if outer and inner:
        kept, refs = refs[:3], refs[3:]
    filtered, refs = refs[0], refs[1:]
    if outer:
        outs, refs = refs[:nx], refs[nx:]
        whole, coef, one, two, three = refs
    else:
        one, two, three, whole, coef = refs
    position = 0
    for ref in ins:
        count = ref.shape[0]
        whole[position : position + count] = ref[...]
        position += count
    zz = position
    zc = zz - 2 * first_state
    shape = whole.shape[2:]
    lanes = shape[-1]
    shifts = Shifts(shape, yl, fields)
    upper = iota(shape, 1) < fields

    def planes_of(margin):
        due = range(margin, zz - margin)
        if kept:
            own = range(first_state + margin, first_state + zc - margin)
            due = [z for z in due if z not in own]
        due = sorted(due, key=lambda z: min(z, zz - 1 - z))
        return due

    for z in sorted({z for margin in (1, 2, 3) for z in planes_of(margin)}):
        nu = whole[z, 1]
        total = None
        for k, other in enumerate((*shifts.pairs(nu), whole[z + 1, 1], whole[z - 1, 1])):
            face = nu + other
            coef[z, k] = face
            total = face if total is None else total + face
        coef[z, 6] = 1.0 - (0.5 * TIME_STEP) * total

    def advanced(load, row, z):
        c = load(z)
        xp, xm, yp, ym = shifts.pairs(c)
        total = None
        for d, (p, m) in enumerate(((xp, xm), (yp, ym), (load(z + 1), load(z - 1)))):
            top = jnp.broadcast_to(row(z, d), shape)
            velocity = jnp.where(upper, top, jnp.broadcast_to(row(z, fields + d), shape))
            term = (coef[z, 2 * d] - velocity) * p + (coef[z, 2 * d + 1] + velocity) * m
            total = term if total is None else total + term
        return c * coef[z, 6] + (0.5 * TIME_STEP) * total

    for z in planes_of(1):
        one[z] = advanced(lambda i: whole[i, 0], lambda i, r: whole[i, 0, :, r : r + 1, :], z)
    if kept:
        for z in (1, 2, zc - 3, zc - 2):
            one[first_state + z] = kept[0][z]
        for z in (2, 3, zc - 4, zc - 3):
            two[first_state + z] = kept[1][z]
        three[first_state + 3 : first_state + zc - 3] = kept[2][3 : zc - 3]
    for z in planes_of(2):
        moved = advanced(lambda i: one[i], lambda i, r: one[i, :, r : r + 1, :], z)
        two[z] = 0.75 * whole[z, 0] + 0.25 * moved
    for z in planes_of(3):
        moved = advanced(lambda i: two[i], lambda i, r: two[i, :, r : r + 1, :], z)
        three[z] = whole[z, 0] * (1.0 / 3.0) + (2.0 / 3.0) * moved

    if outer:
        a, b = lax.axis_index("gx"), lax.axis_index("gy")
        mask = iota((zc // 2, 2 * fields, lanes), 1) < fields
        first = jnp.full((zc // 2, 2 * fields, lanes), b) == 0
        for d in range(nx):
            target = lax.rem(a + d, nx)
            block = three[first_state : first_state + zc, target]
            block = block.reshape(zc // 2, 2, 2 * fields, lanes)
            even, odd = block[:, 0], block[:, 1]
            zero = jnp.where(mask, even, pltpu.roll(odd, fields, 1))
            other = jnp.where(mask, pltpu.roll(even, fields, 1), odd)
            outs[d][0] = jnp.where(first, zero, other).reshape(zc * fields, lanes)
            outs[d][1] = jnp.where(first, other, zero).reshape(zc * fields, lanes)

    for i, plane in enumerate(planes):
        z = first_state + 2 * plane
        s0, s1 = three[z], three[z + 1]
        rows = []
        for value in (s0 + s1, s0 * s0 + s1 * s1):
            value = value + pltpu.roll(value, lanes - yl, 2)
            rows.append(value + pltpu.roll(value, lanes - 1, 2))
        both = jnp.concatenate(rows, axis=1)
        height = both.shape[1]
        for part in range(3):
            rounded = both.astype(BF16)
            both = both - rounded.astype(F32)
            for k in range(shape[0]):
                filtered[
                    i, part * height : (part + 1) * height, k * lanes : (k + 1) * lanes
                ] = rounded[k]


def twice_gelu(x):
    inner = x * (0.7978845608028654 + 0.035677408136300125 * (x * x))
    return x + x * jnp.tanh(inner)


def rms_scale(v, gain):
    total = jnp.sum(v * v, axis=-1, keepdims=True)
    return v * lax.rsqrt(total + EPSILON * v.shape[-1]) * gain


def matmul(v, w):
    return jnp.dot(v, w, preferred_element_type=F32)


def against(v, w):
    return lax.dot_general(v, w, (((1,), (1,)), ((), ())), preferred_element_type=F32)


def attend(section, groups, same, weights, gain):
    qkv_w, out_w = weights
    channels = section.shape[1]
    carried = section.astype(F32)
    normed = rms_scale(carried, gain).astype(BF16)
    yield
    qkv = matmul(normed, qkv_w).astype(BF16)
    yield
    scale = channels ** (-0.5) * 1.4426950408889634
    values, scores = [], []
    for group in groups:
        rows = jnp.concatenate([qkv[s : s + n] for s, n in group], axis=0)
        q, k = rows[:, :channels], rows[:, channels : 2 * channels]
        values.append(rows[:, 2 * channels :])
        scores.append(jnp.where(same, against(q, k), MASKED))
        yield
    weighted = []
    for score in scores:
        exponent = jnp.exp2((score - jnp.max(score, axis=-1, keepdims=True)) * scale)
        weighted.append(exponent.astype(BF16))
        yield
    pieces = {}
    for group, exponent, v in zip(groups, weighted, values):
        summed = matmul(exponent, jnp.concatenate([v, jnp.ones_like(v)], axis=1))
        result = (summed[:, :channels] * (1.0 / summed[:, channels:])).astype(BF16)
        at = 0
        for s, n in group:
            pieces[s] = result[at : at + n]
            at += n
        yield
    attended = jnp.concatenate([pieces[s] for s in sorted(pieces)], axis=0)
    return carried + matmul(attended, out_w)


def feed(residual, weights, gain):
    up_w, down_w = weights
    again = rms_scale(residual, gain).astype(BF16)
    yield
    rows, hidden = residual.shape[0], up_w.shape[1]
    wide, tall = min(256, hidden), min(64, rows)
    total = None
    for h in range(0, hidden, wide):
        up = matmul(again, up_w[:, h : h + wide])
        pieces = []
        for r in range(0, rows, tall):
            pieces.append(twice_gelu(up[r : r + tall].astype(BF16)))
            yield
        down = matmul(jnp.concatenate(pieces, axis=0), down_w[h : h + wide])
        total = down if total is None else total + down
        yield
    return (residual + 0.5 * total).astype(BF16)


def together(tasks):
    results = [None] * len(tasks)
    alive = dict(enumerate(tasks))
    while alive:
        for i in list(alive):
            try:
                next(alive[i])
            except StopIteration as stop:
                results[i] = stop.value
                del alive[i]
    return results


def attention_kernel(nx, ny, fields, cells, step, last, earlier, *refs):
    filtered, sel, lift_w, gains, query_w, key_w, value_w = refs[:7]
    (out_w, up_w, down_w, head), refs = refs[7:11], refs[11:]
    if last:
        if earlier:
            before, refs = refs[0], refs[1:]
        spread, refs = refs[0], refs[1:]
        states, refs = refs[:nx], refs[nx:]
        outs, refs = refs[:nx], refs[nx:]
    coefficient = refs[0]
    xc, yc = cells
    channels = gains.shape[1]
    bias = gains[6:7]
    planes, height, wide = filtered.shape
    side = nx * xc * yc
    per_plane = ny * side
    cut, span = sel.shape
    along_x = [[(b * side, side)] for b in range(ny)]
    count = max(1, 128 // (ny * xc * yc))
    piece = count * xc * yc
    along_y = [
        [(b * side + g * piece, piece) for b in range(ny)] for g in range(nx // count)
    ]
    row, column = iota((side, side), 0), iota((side, side), 1)
    same_x_line = lax.rem(row, yc) == lax.rem(column, yc)
    count = ny * piece
    row, column = iota((count, count), 0), iota((count, count), 1)
    same_y_line = lax.rem(row, piece) // yc == lax.rem(column, piece) // yc
    gain = [gains[i : i + 1] for i in range(6)]
    qkv_w = [
        jnp.concatenate([query_w[i], key_w[i], value_w[i]], axis=1) for i in range(2)
    ]

    def lift_and_first(block):
        by_core = [[] for _ in range(ny)]
        for g in range(wide // span):
            parts = block[:, g * span : (g + 1) * span]
            picked = against(sel[...], jnp.concatenate([parts] * 3, axis=0)).astype(BF16)
            yield
            both = matmul(picked, lift_w[...])
            for b in range(ny):
                by_core[b].append(both[:, b * channels : (b + 1) * channels])
        yield
        features = []
        for rows in sum(by_core, []):
            lifted = rows + bias
            features.append((0.5 * twice_gelu(rms_scale(lifted, gain[0]))).astype(BF16))
            yield
        features = jnp.concatenate(features, axis=0)
        weights = qkv_w[0], out_w[0]
        return (yield from attend(features, along_x, same_x_line, weights, gain[1]))

    def first_feed(residual):
        return feed(residual, (up_w[0], down_w[0]), gain[2])

    def second(value):
        return attend(value, along_y, same_y_line, (qkv_w[1], out_w[1]), gain[3])

    def second_feed_and_head(residual, turned, plus):
        value = yield from feed(residual, (up_w[1], down_w[1]), gain[4])
        final = rms_scale(value.astype(F32), gain[5]).astype(BF16)
        yield
        logits = against(turned, final)
        return logits if plus is None else logits + plus

    def coefficient_of(logits):
        return 0.05 + 0.45 * jax.nn.sigmoid(logits)

    def chain(plane, turned):
        value = yield from lift_and_first(plane)
        value = yield from first_feed(value)
        value = yield from second(value)
        return (yield from second_feed_and_head(value, turned, None))

    def some_planes(i, carry):
        tasks = [chain(filtered[i * width + p], head[p % step]) for p in range(width)]
        found = together(tasks)
        for p in range(0, width, step):
            row = i * (width // step) + p // step
            coefficient[row] = coefficient_of(sum(found[p + 1 : p + step], found[p]))
        return carry

    width = planes if planes * per_plane <= 2048 else step
    lax.fori_loop(0, planes // width, some_planes, 0)

    if last:
        a, b = lax.axis_index("gx"), lax.axis_index("gy")
        every = coefficient[...].reshape(-1, per_plane)
        if earlier:
            every = jnp.concatenate([before[...].reshape(-1, per_plane), every], axis=0)
        kept = 2 * states[0].shape[1]
        depth = outs[0].shape[1] - kept
        if every.shape[0] < depth:
            blank = jnp.zeros((depth - every.shape[0], per_plane), F32)
            every = jnp.concatenate([every, blank], axis=0)
        every = every.astype(BF16).astype(F32)
        width = spread.shape[1] // ny
        first = jnp.full((depth, width), b) == 0
        for d in range(nx):
            target = lax.rem(a + d, nx)
            shift = lax.rem((nx + 1 - target) * (xc * yc), side)
            near = [
                pltpu.roll(every[:, k * side : (k + 1) * side], shift, 1)[:, :cut]
                for k in range(ny)
            ]
            near = jnp.concatenate(near, axis=1).astype(BF16)
            found = matmul(near, spread[...])
            zero, other = found[:, :width], found[:, width:]
            high, low = halves(states[d][...])
            outs[d][:, : kept // 2] = high
            outs[d][:, kept // 2 : kept] = low
            outs[d][0, kept:] = jnp.where(first, zero, other).astype(BF16)
            outs[d][1, kept:] = jnp.where(first, other, zero).astype(BF16)


def return_kernel(nx, ny, mine, got, along_z, across, *refs):
    state_out, eddy_out, state_rows, coarse_rows, state, eddy, sems = refs
    fields, xl, yl, zl = state_out.shape
    a, b = lax.axis_index("gx"), lax.axis_index("gy")
    size = state_rows.shape[0] // (nx * ny)
    for d in range(nx):
        for piece, core in ((mine, b), (got, lax.rem(b + 1, ny))):
            chunk = lax.rem(a + nx - d, nx) * ny + core
            start = pl.multiple_of(chunk * size, 8)
            high, low = piece[d, :size].astype(F32), piece[d, size : 2 * size].astype(F32)
            state_rows[pl.ds(start, size), :] = high + low
            coarse_rows[chunk] = piece[d, 2 * size :]
    copies = []

    def send(buffer, out, f):
        copy = pltpu.make_async_copy(buffer.at[f], out.at[f], sems.at[len(copies)])
        copy.start()
        copies.append(copy)

    for f in range(fields):
        rows = state_rows[pl.ds(f, zl, stride=fields), :]
        state[f] = rows.T.reshape(xl, yl, zl)
        send(state, state_out, f)
    count, depth, width = coarse_rows.shape
    coarse = coarse_rows[...].reshape(count * depth, width)
    for f in range(fields):
        spread = lax.dot_general(
            coarse,
            along_z[:, f * zl : (f + 1) * zl],
            (((0,), (0,)), ((), ())),
            preferred_element_type=F32,
        )
        total = None
        for part in range(3):
            rounded = spread.astype(BF16)
            spread = spread - rounded.astype(F32)
            product = matmul(across[...], rounded)
            total = product if total is None else total + product
        eddy[f] = total.reshape(xl, yl, zl)
        send(eddy, eddy_out, f)
    for copy in copies:
        copy.wait()


def pick_matrix(group, xl, yl):
    xc, yc = xl // 2, yl // 2
    table = np.zeros((group, xl, yl, group, xc, yc), np.float32)
    for k in range(group):
        for x in range(xc):
            for y in range(yc):
                table[k, 2 * x, 2 * y, k, x, y] = 0.125
    return table.reshape(group * xl * yl, group * xc * yc)


def spread_matrix(ny, near, xc, yc, width):
    table = np.zeros((ny, near, xc, yc, ny, width), np.float32)
    for target in range(ny):
        for i in range(xc + 2):
            x = i - 1 + xc
            for j in range(yc + 2):
                y = (target * yc + j - 1) % (ny * yc)
                table[y // yc, x // xc, x % xc, y % yc, target, i * (yc + 2) + j] = 1.0
    return table.reshape(ny * near * xc * yc, ny * width)


def taps(fine):
    return ((fine // 2, 0.75), (fine // 2 + (1 if fine % 2 else -1), 0.25))


def across_matrix(xl, yl, width):
    yc = yl // 2
    table = np.zeros((xl, yl, width), np.float32)
    for x in range(xl):
        for y in range(yl):
            for i, u in taps(x):
                for j, v in taps(y):
                    table[x, y, (i + 1) * (yc + 2) + j + 1] += u * v
    return table.reshape(xl * yl, width)


def along_z_matrix(chunks, depth, place, fields, zc):
    table = np.zeros((chunks, depth, fields, chunks, zc), np.float32)
    for c in range(chunks):
        for z in range(zc):
            for i, u in taps(z):
                for f in range(fields):
                    table[c, place[i] + f, f, c, z] += u
    return table.reshape(chunks * depth, fields * chunks * zc)


def exchange(messages, nx, ny, meanwhile=()):
    received = [messages[0]] + [None] * (nx - 1)
    for d in sorted(range(1, nx), key=lambda d: abs(2 * d - nx)):
        received[d] = lax.ppermute(messages[d], "gx", [(i, (i + d) % nx) for i in range(nx)])
    shape = (nx,) + messages[0].shape[1:]
    mine, away = call(
        functools.partial(sort_kernel, nx),
        [(shape, messages[0].dtype)] * 2,
        [*received, *meanwhile],
        flops=1000,
        moved=8 * math.prod(shape),
    )
    return mine, lax.ppermute(away, "gy", [(i, (i + 1) % ny) for i in range(ny)])


def per_device(
    nx,
    ny,
    nz,
    flow_state,
    viscosity,
    lift_weight,
    lift_bias,
    norm_gains,
    query_weight,
    key_weight,
    value_weight,
    output_weight,
    up_weight,
    down_weight,
    head_weight,
):
    fields, xl, yl, zl = flow_state.shape
    lanes = xl * yl
    chunks = nx * ny
    zc = zl // chunks
    half = zc // 2
    xc, yc = xl // 2, yl // 2
    channels = lift_bias.shape[0]
    hidden = up_weight.shape[-1]
    both = 2 * fields
    per_plane = chunks * xc * yc

    group = max(1, 512 // lanes)
    sel = jnp.asarray(pick_matrix(group, xl, yl).T, BF16)
    small, lift_w, head_w = call(
        functools.partial(small_kernel, ny, fields),
        [
            ((8, channels), F32),
            ((9 * 2 * ny * fields, ny * channels), BF16),
            ((2, 8, channels), BF16),
        ],
        [lift_weight, lift_bias.reshape(1, channels), norm_gains, head_weight],
        flops=1000000,
        moved=200000,
    )

    packed = call(
        functools.partial(pack_kernel, nx, ny),
        [((ny, 3, zc * fields, lanes), BF16)] * nx,
        [flow_state, viscosity],
        [
            pltpu.VMEM((2, zl * fields, lanes), F32),
            pltpu.VMEM((both, xl, yl, zl), F32),
            pltpu.SemaphoreType.DMA((both,)),
        ],
        flops=1000000,
        moved=4 * zl * both * lanes,
        room=53.5,
        where=(HBM, VMEM),
    )
    mine, got = exchange(packed, nx, ny, [small])
    ring = []
    while sum(ring) < HALO:
        ring.append(min(zc, HALO - sum(ring)))
    block = (2, nx, ny * fields, lanes)
    unified = call(
        functools.partial(unify_kernel, nx, fields, ring),
        [((zc,) + block, F32)] + [((n,) + block, F32) for n in ring for _ in range(2)],
        [mine, got],
        flops=1000000,
        moved=8 * zl * both * lanes,
    )
    own, ends = unified[0], unified[1:]
    total = nz * chunks

    def ring_step(value, move):
        pairs = []
        for k in range(total):
            t = (k + move) % total
            pairs.append(((k % chunks) * nz + k // chunks, (t % chunks) * nz + t // chunks))
        return lax.ppermute(value, ("gx", "gy", "gz"), pairs)

    above = [ring_step(ends[2 * s], -(s + 1)) for s in range(len(ring))]
    below = [ring_step(ends[2 * s + 1], s + 1) for s in range(len(ring))]

    inner = list(range(2, half - 2))
    outer = [p for p in range(-1, half + 1) if p not in inner]

    def stencil(inputs, first_state, planes, kept, last):
        zz = sum(v.shape[0] for v in inputs)
        size = ((zz,) + block[1:], F32)
        outs = [((len(planes), 3 * 2 * ny * fields, nx * lanes), BF16)]
        outs += [((ny, zc * fields, lanes), F32)] * nx if last else [size] * 3
        return call(
            functools.partial(
                stencil_kernel,
                nx,
                ny,
                fields,
                yl,
                len(inputs),
                first_state,
                planes,
                bool(kept) or not last,
                last,
            ),
            outs,
            [*inputs, *kept],
            [pltpu.VMEM((zz,) + block, F32), pltpu.VMEM((zz, 7) + block[1:], F32)]
            + ([pltpu.VMEM(*size)] * 3 if last else []),
            flops=300000000,
            moved=8 * zz * nx * 8 * lanes,
            room=16 * (nx // 4) ** 2,
        )

    def pairing(planes):
        return 2 if len(planes) % 2 == 0 else 1

    def attention(filtered, planes, more, outs, last):
        step = pairing(planes)
        args = [
            filtered,
            sel,
            lift_w,
            small,
            query_weight,
            key_weight,
            value_weight,
            output_weight,
            up_weight,
            down_weight,
            head_w,
        ] + more
        size = (len(planes) // step, 8, per_plane)
        work = len(planes) * per_plane * channels * (8 * channels + 4 * hidden) * 2
        return call(
            functools.partial(
                attention_kernel, nx, ny, fields, (xc, yc), step, last, bool(last and inner)
            ),
            outs if last else [(size, F32)],
            args,
            ([pltpu.VMEM(size, F32)] if last else []),
            flops=3 * work,
            moved=1000000,
            room=16 * (nx // 4) ** 2,
        )

    place = {}
    depth = 0
    for planes in (inner, outer):
        step = pairing(planes)
        for i, p in enumerate(planes):
            place[p] = depth + (i // step) * 8 + (i % step) * fields
        depth += len(planes) // step * 8
    depth = -(-depth // 16) * 16

    more, kept = [], []
    if inner:
        filtered, *kept = stencil([own], 0, inner, [], False)
        more = list(attention(filtered, inner, [], None, False))

    ordered = below[::-1] + [own] + above
    second = stencil(ordered, HALO, outer, kept, True)
    filtered, state_messages = second[0], list(second[1:])

    width = -(-(xc + 2) * (yc + 2) // 128) * 128
    near = 128 // (xc * yc)
    spread = jnp.asarray(spread_matrix(ny, near, xc, yc, width), BF16)
    rows = zc * fields
    messages = attention(
        filtered,
        outer,
        more + [spread] + state_messages,
        [((ny, 2 * rows + depth, width), BF16)] * nx,
        True,
    )
    mine, got = exchange(list(messages), nx, ny)
    along_z = jnp.asarray(along_z_matrix(chunks, depth, place, fields, zc), BF16)
    across = jnp.asarray(across_matrix(xl, yl, width), BF16)
    state_next, eddy_field = call(
        functools.partial(return_kernel, nx, ny),
        [(flow_state.shape, F32)] * 2,
        [mine, got, along_z, across],
        [
            pltpu.VMEM((zl * fields, lanes), F32),
            pltpu.VMEM((chunks, depth, width), BF16),
            pltpu.VMEM(flow_state.shape, F32),
            pltpu.VMEM(flow_state.shape, F32),
            pltpu.SemaphoreType.DMA((2 * fields,)),
        ],
        flops=1000000,
        moved=8 * zl * fields * lanes,
        where=(VMEM, HBM),
    )
    return (state_next, eddy_field)


def solution(mesh):
    sizes = [mesh.shape[name] for name in ("gx", "gy", "gz")]
    return jax.shard_map(
        functools.partial(per_device, *sizes),
        mesh=mesh,
        in_specs=(
            P(None, "gx", "gy", "gz"),
            P(None, "gx", "gy", "gz"),
            P(),
            P(),
            P(),
            P(),
            P(),
            P(),
            P(),
            P(),
            P(),
            P(),
        ),
        out_specs=(P(None, "gx", "gy", "gz"), P(None, "gx", "gy", "gz")),
        check_vma=False,
    )
```

```python
import functools
import math

import jax
import jax.numpy as jnp
import numpy as np
from jax import lax
from jax.experimental import pallas as pl
from jax.experimental.pallas import tpu as pltpu
from jax.sharding import PartitionSpec as P

EPSILON = 1e-06
TIME_STEP = 0.3
HALO = 5
EXTRA = 1000
MASKED = -1e30
MIDDLE, REACH, OCTAVES = 0.275, 0.225, 118.0
F32 = jnp.float32
BF16 = jnp.bfloat16
VMEM = pl.BlockSpec(memory_space=pltpu.VMEM)
HBM = pl.BlockSpec(memory_space=pltpu.HBM)


def call(body, outs, args, scratch=(), flops=0, moved=0, room=16, where=(VMEM, VMEM)):
    return pl.pallas_call(
        body,
        out_shape=tuple(jax.ShapeDtypeStruct(s, d) for s, d in outs),
        in_specs=[where[0]] * len(args),
        out_specs=tuple([where[1]] * len(outs)),
        scratch_shapes=list(scratch),
        cost_estimate=pl.CostEstimate(flops=flops, bytes_accessed=moved, transcendentals=0),
        compiler_params=pltpu.CompilerParams(vmem_limit_bytes=int(min(room, 63.93) * 1048576)),
    )(*args)


def iota(shape, dim):
    return lax.broadcasted_iota(jnp.int32, shape, dim)


def halves(v):
    high = v.astype(BF16)
    return high, (v - high.astype(F32)).astype(BF16)


def coded(nu):
    place = (nu - MIDDLE) * (OCTAVES / REACH)
    size = jnp.exp2(2.0 * jnp.abs(place) - OCTAVES)
    return jnp.where(place < 0.0, -size, size).astype(BF16)


def decoded(code):
    size = (jnp.log2(jnp.abs(code)) + OCTAVES) * (0.5 * REACH / OCTAVES)
    return MIDDLE + jnp.where(code < 0.0, -size, size)


def pack_kernel(nx, ny, flow, visc, *rest):
    outs, (turned, blocks, sems) = rest[:nx], rest[nx:]
    fields, xl, yl, zl = flow.shape
    lanes = xl * yl
    both = 2 * fields
    copies = []
    for f in range(both):
        source = flow.at[f] if f < fields else visc.at[f - fields]
        copies.append(pltpu.make_async_copy(source, blocks.at[f], sems.at[f]))
        copies[f].start()
    for f in range(both):
        copies[f].wait()
        kind, row = divmod(f, fields)
        turned[kind, pl.ds(row, zl, stride=fields), :] = blocks[f].reshape(lanes, zl).T
    rows = zl * fields // (nx * ny)
    a, b = lax.axis_index("gx"), lax.axis_index("gy")
    for d in range(nx):
        for e in range(ny):
            chunk = lax.rem(a + d, nx) * ny + lax.rem(b + e, ny)
            start = pl.multiple_of(chunk * rows, 8)
            high, low = halves(turned[0, pl.ds(start, rows), :])
            outs[d][e, 0] = high
            outs[d][e, 1] = low
            outs[d][e, 2] = coded(turned[1, pl.ds(start, rows), :])


def small_kernel(ny, fields, lift, bias, gains, head, small, lift_w, head_w):
    channels = gains.shape[1]
    small[:6] = gains[...] * channels**0.5
    small[6:7] = bias[...]
    small[7:8] = bias[...]
    rest = lift[...]
    rows = rest.shape[0]
    upper = lax.rem(iota((rows, channels), 0), 2 * fields) < fields
    for part in range(3):
        rounded = rest.astype(BF16)
        rest = rest - rounded.astype(F32)
        exact = rounded.astype(F32)
        swapped = pltpu.roll(exact, fields, 0)
        for b in range(ny):
            first = exact if b == 0 else swapped
            second = swapped if b == 0 else exact
            keep = upper if b == 0 else jnp.logical_not(upper)
            both = jnp.concatenate(
                [jnp.where(keep, first, 0.0), jnp.where(keep, second, 0.0)], axis=0
            ).astype(BF16)
            for again in range(3):
                at = (part * 3 + again) * 2 * rows
                lift_w[at : at + 2 * rows, b * channels : (b + 1) * channels] = both
    turned = head[...].astype(F32).T
    turned = jnp.concatenate([turned, jnp.zeros_like(turned)], axis=0)
    head_w[0] = turned.astype(BF16)
    head_w[1] = pltpu.roll(turned, fields, 0).astype(BF16)


def sort_kernel(nx, *refs):
    parts, (mine, away) = refs[:nx], refs[-2:]
    for d in range(nx):
        mine[d] = parts[d][0]
        away[d] = parts[d][1]


def unify_kernel(nx, fields, ring, mine, got, whole, *ends):
    a, b = lax.axis_index("gx"), lax.axis_index("gy")
    rows, lanes = got.shape[2:]
    zc = rows // fields
    shape = zc // 2, 2 * fields, lanes
    low = iota(shape, 1) < fields
    first = jnp.full(shape, b) == 0
    for d in range(nx):
        where_from = lax.rem(a + nx - d, nx)
        near = mine[d].astype(F32)
        far = got[d].astype(F32)
        for kind in range(2):
            m = (decoded(near[2]) if kind else near[0] + near[1]).reshape(shape)
            t = (decoded(far[2]) if kind else far[0] + far[1]).reshape(shape)
            p = jnp.where(first, m, t)
            q = jnp.where(first, t, m)
            even = jnp.where(low, p, pltpu.roll(q, fields, 1))
            odd = jnp.where(low, pltpu.roll(p, fields, 1), q)
            for z in range(zc // 2):
                whole[2 * z, kind, where_from] = even[z]
                whole[2 * z + 1, kind, where_from] = odd[z]
    for s, count in enumerate(ring):
        ends[2 * s][...] = whole[:count]
        ends[2 * s + 1][...] = whole[zc - count :]


class Shifts:
    def __init__(self, shape, yl, fields):
        self.lanes, self.yl, self.fields = shape[-1], yl, fields
        lane = iota(shape, 2)
        self.last_x = lane >= self.lanes - yl
        self.first_x = lane < yl
        inner = lax.rem(lane, yl)
        self.last_y = inner == yl - 1
        self.first_y = inner == 0

    def pairs(self, v):
        n, yl = self.lanes, self.yl
        r = pltpu.roll(v, n - yl, 2)
        xp = jnp.where(self.last_x, jnp.concatenate([r[1:], r[:1]], 0), r)
        r = pltpu.roll(v, yl, 2)
        xm = jnp.where(self.first_x, jnp.concatenate([r[-1:], r[:-1]], 0), r)
        other = pltpu.roll(v, self.fields, 1)
        yp = jnp.where(self.last_y, pltpu.roll(other, yl - 1, 2), pltpu.roll(v, n - 1, 2))
        ym = jnp.where(self.first_y, pltpu.roll(other, n - yl + 1, 2), pltpu.roll(v, 1, 2))
        return xp, xm, yp, ym


def stencil_kernel(nx, ny, fields, yl, blocks, first_state, planes, inner, outer, *refs):
    ins, refs = refs[:blocks], refs[blocks:]
    kept = ()
    if outer and inner:
        kept, refs = refs[:3], refs[3:]
    filtered, refs = refs[0], refs[1:]
    if outer:
        outs, refs = refs[:nx], refs[nx:]
        whole, coef, one, two, three = refs
    else:
        one, two, three, whole, coef = refs
    position = 0
    for ref in ins:
        count = ref.shape[0]
        whole[position : position + count] = ref[...]
        position += count
    zz = position
    zc = zz - 2 * first_state
    shape = whole.shape[2:]
    lanes = shape[-1]
    shifts = Shifts(shape, yl, fields)
    upper = iota(shape, 1) < fields

    def planes_of(margin):
        due = range(margin, zz - margin)
        if kept:
            own = range(first_state + margin, first_state + zc - margin)
            due = [z for z in due if z not in own]
        due = sorted(due, key=lambda z: min(z, zz - 1 - z))
        return due

    for z in sorted({z for margin in (1, 2, 3) for z in planes_of(margin)}):
        nu = whole[z, 1]
        total = None
        for k, other in enumerate((*shifts.pairs(nu), whole[z + 1, 1], whole[z - 1, 1])):
            face = nu + other
            coef[z, k] = face
            total = face if total is None else total + face
        coef[z, 6] = 1.0 - (0.5 * TIME_STEP) * total

    def advanced(load, row, z):
        c = load(z)
        xp, xm, yp, ym = shifts.pairs(c)
        total = None
        for d, (p, m) in enumerate(((xp, xm), (yp, ym), (load(z + 1), load(z - 1)))):
            top = jnp.broadcast_to(row(z, d), shape)
            velocity = jnp.where(upper, top, jnp.broadcast_to(row(z, fields + d), shape))
            term = (coef[z, 2 * d] - velocity) * p + (coef[z, 2 * d + 1] + velocity) * m
            total = term if total is None else total + term
        return c * coef[z, 6] + (0.5 * TIME_STEP) * total

    for z in planes_of(1):
        one[z] = advanced(lambda i: whole[i, 0], lambda i, r: whole[i, 0, :, r : r + 1, :], z)
    if kept:
        for z in (1, 2, zc - 3, zc - 2):
            one[first_state + z] = kept[0][z]
        for z in (2, 3, zc - 4, zc - 3):
            two[first_state + z] = kept[1][z]
        three[first_state + 3 : first_state + zc - 3] = kept[2][3 : zc - 3]
    for z in planes_of(2):
        moved = advanced(lambda i: one[i], lambda i, r: one[i, :, r : r + 1, :], z)
        two[z] = 0.75 * whole[z, 0] + 0.25 * moved
    for z in planes_of(3):
        moved = advanced(lambda i: two[i], lambda i, r: two[i, :, r : r + 1, :], z)
        three[z] = whole[z, 0] * (1.0 / 3.0) + (2.0 / 3.0) * moved

    if outer:
        a, b = lax.axis_index("gx"), lax.axis_index("gy")
        mask = iota((zc // 2, 2 * fields, lanes), 1) < fields
        first = jnp.full((zc // 2, 2 * fields, lanes), b) == 0
        for d in range(nx):
            target = lax.rem(a + d, nx)
            block = three[first_state : first_state + zc, target]
            block = block.reshape(zc // 2, 2, 2 * fields, lanes)
            even, odd = block[:, 0], block[:, 1]
            zero = jnp.where(mask, even, pltpu.roll(odd, fields, 1))
            other = jnp.where(mask, pltpu.roll(even, fields, 1), odd)
            outs[d][0] = jnp.where(first, zero, other).reshape(zc * fields, lanes)
            outs[d][1] = jnp.where(first, other, zero).reshape(zc * fields, lanes)

    chunk = lax.axis_index("gx") * ny + lax.axis_index("gy")
    for i, plane in enumerate(planes):
        z = first_state + 2 * plane
        if plane == EXTRA:
            z = first_state + jnp.where(chunk < nx * ny // 2, -2, zc)
        s0, s1 = three[z], three[z + 1]
        rows = []
        for value in (s0 + s1, s0 * s0 + s1 * s1):
            value = value + pltpu.roll(value, lanes - yl, 2)
            rows.append(value + pltpu.roll(value, lanes - 1, 2))
        both = jnp.concatenate(rows, axis=1)
        height = both.shape[1]
        for part in range(3):
            rounded = both.astype(BF16)
            both = both - rounded.astype(F32)
            for k in range(shape[0]):
                filtered[
                    i, part * height : (part + 1) * height, k * lanes : (k + 1) * lanes
                ] = rounded[k]


def twice_gelu(x):
    inner = x * (0.7978845608028654 + 0.035677408136300125 * (x * x))
    return x + x * jnp.tanh(inner)


def rms_scale(v, gain):
    total = jnp.sum(v * v, axis=-1, keepdims=True)
    return v * lax.rsqrt(total + EPSILON * v.shape[-1]) * gain


def matmul(v, w):
    return jnp.dot(v, w, preferred_element_type=F32)


def against(v, w):
    return lax.dot_general(v, w, (((1,), (1,)), ((), ())), preferred_element_type=F32)


def attend(section, groups, same, weights, gain):
    qkv_w, out_w = weights
    channels = section.shape[1]
    carried = section.astype(F32)
    normed = rms_scale(carried, gain).astype(BF16)
    yield
    qkv = matmul(normed, qkv_w).astype(BF16)
    yield
    scale = channels ** (-0.5) * 1.4426950408889634
    values, scores = [], []
    for group in groups:
        rows = jnp.concatenate([qkv[s : s + n] for s, n in group], axis=0)
        q, k = rows[:, :channels], rows[:, channels : 2 * channels]
        values.append(rows[:, 2 * channels :])
        scores.append(jnp.where(same, against(q, k), MASKED))
        yield
    weighted = []
    for score in scores:
        exponent = jnp.exp2((score - jnp.max(score, axis=-1, keepdims=True)) * scale)
        weighted.append(exponent.astype(BF16))
        yield
    pieces = {}
    for group, exponent, v in zip(groups, weighted, values):
        summed = matmul(exponent, jnp.concatenate([v, jnp.ones_like(v)], axis=1))
        result = (summed[:, :channels] * (1.0 / summed[:, channels:])).astype(BF16)
        at = 0
        for s, n in group:
            pieces[s] = result[at : at + n]
            at += n
        yield
    attended = jnp.concatenate([pieces[s] for s in sorted(pieces)], axis=0)
    return carried + matmul(attended, out_w)


def feed(residual, weights, gain):
    up_w, down_w = weights
    again = rms_scale(residual, gain).astype(BF16)
    yield
    rows, hidden = residual.shape[0], up_w.shape[1]
    wide, tall = min(256, hidden), min(64, rows)
    total = None
    for h in range(0, hidden, wide):
        up = matmul(again, up_w[:, h : h + wide])
        pieces = []
        for r in range(0, rows, tall):
            pieces.append(twice_gelu(up[r : r + tall].astype(BF16)))
            yield
        down = matmul(jnp.concatenate(pieces, axis=0), down_w[h : h + wide])
        total = down if total is None else total + down
        yield
    return (residual + 0.5 * total).astype(BF16)


def together(tasks):
    results = [None] * len(tasks)
    alive = dict(enumerate(tasks))
    while alive:
        for i in list(alive):
            try:
                next(alive[i])
            except StopIteration as stop:
                results[i] = stop.value
                del alive[i]
    return results


def attention_kernel(nx, ny, fields, cells, step, last, earlier, *refs):
    filtered, sel, lift_w, gains, query_w, key_w, value_w = refs[:7]
    (out_w, up_w, down_w, head), refs = refs[7:11], refs[11:]
    if last:
        if earlier:
            before, refs = refs[0], refs[1:]
        spread, refs = refs[0], refs[1:]
        states, refs = refs[:nx], refs[nx:]
        outs, refs = refs[:nx], refs[nx:]
    coefficient = refs[0]
    xc, yc = cells
    channels = gains.shape[1]
    bias = gains[6:7]
    planes, height, wide = filtered.shape
    side = nx * xc * yc
    per_plane = ny * side
    cut, span = sel.shape
    along_x = [[(b * side, side)] for b in range(ny)]
    count = max(1, 128 // (ny * xc * yc))
    piece = count * xc * yc
    along_y = [
        [(b * side + g * piece, piece) for b in range(ny)] for g in range(nx // count)
    ]
    row, column = iota((side, side), 0), iota((side, side), 1)
    same_x_line = lax.rem(row, yc) == lax.rem(column, yc)
    count = ny * piece
    row, column = iota((count, count), 0), iota((count, count), 1)
    same_y_line = lax.rem(row, piece) // yc == lax.rem(column, piece) // yc
    gain = [gains[i : i + 1] for i in range(6)]
    qkv_w = [
        jnp.concatenate([query_w[i], key_w[i], value_w[i]], axis=1) for i in range(2)
    ]

    def lift_and_first(block):
        by_core = [[] for _ in range(ny)]
        for g in range(wide // span):
            parts = block[:, g * span : (g + 1) * span]
            picked = against(sel[...], jnp.concatenate([parts] * 3, axis=0)).astype(BF16)
            yield
            both = matmul(picked, lift_w[...])
            for b in range(ny):
                by_core[b].append(both[:, b * channels : (b + 1) * channels])
        yield
        features = []
        for rows in sum(by_core, []):
            lifted = rows + bias
            features.append((0.5 * twice_gelu(rms_scale(lifted, gain[0]))).astype(BF16))
            yield
        features = jnp.concatenate(features, axis=0)
        weights = qkv_w[0], out_w[0]
        return (yield from attend(features, along_x, same_x_line, weights, gain[1]))

    def first_feed(residual):
        return feed(residual, (up_w[0], down_w[0]), gain[2])

    def second(value):
        return attend(value, along_y, same_y_line, (qkv_w[1], out_w[1]), gain[3])

    def second_feed_and_head(residual, turned, plus):
        value = yield from feed(residual, (up_w[1], down_w[1]), gain[4])
        final = rms_scale(value.astype(F32), gain[5]).astype(BF16)
        yield
        logits = against(turned, final)
        return logits if plus is None else logits + plus

    def coefficient_of(logits):
        return 0.05 + 0.45 * jax.nn.sigmoid(logits)

    def chain(plane, turned):
        value = yield from lift_and_first(plane)
        value = yield from first_feed(value)
        value = yield from second(value)
        return (yield from second_feed_and_head(value, turned, None))

    def some_planes(i, carry):
        tasks = [chain(filtered[i * width + p], head[p % step]) for p in range(width)]
        found = together(tasks)
        for p in range(0, width, step):
            row = i * (width // step) + p // step
            coefficient[row] = coefficient_of(sum(found[p + 1 : p + step], found[p]))
        return carry

    width = planes if planes * per_plane <= 2048 else step
    lax.fori_loop(0, planes // width, some_planes, 0)

    if last:
        a, b = lax.axis_index("gx"), lax.axis_index("gy")
        every = coefficient[...].reshape(-1, per_plane)
        if earlier:
            every = jnp.concatenate([before[...].reshape(-1, per_plane), every], axis=0)
        kept = 2 * states[0].shape[1]
        depth = outs[0].shape[1] - kept
        if every.shape[0] < depth:
            blank = jnp.zeros((depth - every.shape[0], per_plane), F32)
            every = jnp.concatenate([every, blank], axis=0)
        every = every.astype(BF16).astype(F32)
        width = spread.shape[1] // ny
        first = jnp.full((depth, width), b) == 0
        for d in range(nx):
            target = lax.rem(a + d, nx)
            shift = lax.rem((nx + 1 - target) * (xc * yc), side)
            near = [
                pltpu.roll(every[:, k * side : (k + 1) * side], shift, 1)[:, :cut]
                for k in range(ny)
            ]
            near = jnp.concatenate(near, axis=1).astype(BF16)
            found = matmul(near, spread[...])
            zero, other = found[:, :width], found[:, width:]
            high, low = halves(states[d][...])
            outs[d][:, : kept // 2] = high
            outs[d][:, kept // 2 : kept] = low
            outs[d][0, kept:] = jnp.where(first, zero, other).astype(BF16)
            outs[d][1, kept:] = jnp.where(first, other, zero).astype(BF16)


def return_kernel(nx, ny, mine, got, along_z, across, *refs):
    state_out, eddy_out, state_rows, coarse_rows, state, eddy, sems = refs
    fields, xl, yl, zl = state_out.shape
    a, b = lax.axis_index("gx"), lax.axis_index("gy")
    size = state_rows.shape[0] // (nx * ny)
    for d in range(nx):
        for piece, core in ((mine, b), (got, lax.rem(b + 1, ny))):
            chunk = lax.rem(a + nx - d, nx) * ny + core
            start = pl.multiple_of(chunk * size, 8)
            high, low = piece[d, :size].astype(F32), piece[d, size : 2 * size].astype(F32)
            state_rows[pl.ds(start, size), :] = high + low
            coarse_rows[chunk] = piece[d, 2 * size :]
    copies = []

    def send(buffer, out, f):
        copy = pltpu.make_async_copy(buffer.at[f], out.at[f], sems.at[len(copies)])
        copy.start()
        copies.append(copy)

    for f in range(fields):
        rows = state_rows[pl.ds(f, zl, stride=fields), :]
        state[f] = rows.T.reshape(xl, yl, zl)
        send(state, state_out, f)
    count, depth, width = coarse_rows.shape
    coarse = coarse_rows[...].reshape(count * depth, width)
    for f in range(fields):
        spread = lax.dot_general(
            coarse,
            along_z[:, f * zl : (f + 1) * zl],
            (((0,), (0,)), ((), ())),
            preferred_element_type=F32,
        )
        total = None
        for part in range(3):
            rounded = spread.astype(BF16)
            spread = spread - rounded.astype(F32)
            product = matmul(across[...], rounded)
            total = product if total is None else total + product
        eddy[f] = total.reshape(xl, yl, zl)
        send(eddy, eddy_out, f)
    for copy in copies:
        copy.wait()


def pick_matrix(group, xl, yl):
    xc, yc = xl // 2, yl // 2
    table = np.zeros((group, xl, yl, group, xc, yc), np.float32)
    for k in range(group):
        for x in range(xc):
            for y in range(yc):
                table[k, 2 * x, 2 * y, k, x, y] = 0.125
    return table.reshape(group * xl * yl, group * xc * yc)


def spread_matrix(ny, near, xc, yc, width):
    table = np.zeros((ny, near, xc, yc, ny, width), np.float32)
    for target in range(ny):
        for i in range(xc + 2):
            x = i - 1 + xc
            for j in range(yc + 2):
                y = (target * yc + j - 1) % (ny * yc)
                table[y // yc, x // xc, x % xc, y % yc, target, i * (yc + 2) + j] = 1.0
    return table.reshape(ny * near * xc * yc, ny * width)


def taps(fine):
    return ((fine // 2, 0.75), (fine // 2 + (1 if fine % 2 else -1), 0.25))


def across_matrix(xl, yl, width):
    yc = yl // 2
    table = np.zeros((xl, yl, width), np.float32)
    for x in range(xl):
        for y in range(yl):
            for i, u in taps(x):
                for j, v in taps(y):
                    table[x, y, (i + 1) * (yc + 2) + j + 1] += u * v
    return table.reshape(xl * yl, width)


def along_z_matrix(chunks, depth, place, fields, zc):
    half = zc // 2
    table = np.zeros((chunks, depth, fields, chunks * zc), np.float32)
    for z in range(chunks * zc):
        for i, u in taps(z):
            if 0 <= i < chunks * half:
                c, row = i // half, place[i % half]
            else:
                c, row = (0 if i < 0 else chunks - 1), place[EXTRA]
            for f in range(fields):
                table[c, row + f, f, z] += u
    return table.reshape(chunks * depth, fields * chunks * zc)


def exchange(messages, nx, ny, meanwhile=()):
    received = [messages[0]] + [None] * (nx - 1)
    for d in sorted(range(1, nx), key=lambda d: abs(2 * d - nx)):
        received[d] = lax.ppermute(messages[d], "gx", [(i, (i + d) % nx) for i in range(nx)])
    shape = (nx,) + messages[0].shape[1:]
    mine, away = call(
        functools.partial(sort_kernel, nx),
        [(shape, messages[0].dtype)] * 2,
        [*received, *meanwhile],
        flops=1000,
        moved=8 * math.prod(shape),
    )
    return mine, lax.ppermute(away, "gy", [(i, (i + 1) % ny) for i in range(ny)])


def per_device(
    nx,
    ny,
    nz,
    flow_state,
    viscosity,
    lift_weight,
    lift_bias,
    norm_gains,
    query_weight,
    key_weight,
    value_weight,
    output_weight,
    up_weight,
    down_weight,
    head_weight,
):
    fields, xl, yl, zl = flow_state.shape
    lanes = xl * yl
    chunks = nx * ny
    zc = zl // chunks
    half = zc // 2
    xc, yc = xl // 2, yl // 2
    channels = lift_bias.shape[0]
    hidden = up_weight.shape[-1]
    both = 2 * fields
    per_plane = chunks * xc * yc

    group = max(1, 512 // lanes)
    sel = jnp.asarray(pick_matrix(group, xl, yl).T, BF16)
    small, lift_w, head_w = call(
        functools.partial(small_kernel, ny, fields),
        [
            ((8, channels), F32),
            ((9 * 2 * ny * fields, ny * channels), BF16),
            ((2, 8, channels), BF16),
        ],
        [lift_weight, lift_bias.reshape(1, channels), norm_gains, head_weight],
        flops=1000000,
        moved=200000,
    )

    packed = call(
        functools.partial(pack_kernel, nx, ny),
        [((ny, 3, zc * fields, lanes), BF16)] * nx,
        [flow_state, viscosity],
        [
            pltpu.VMEM((2, zl * fields, lanes), F32),
            pltpu.VMEM((both, xl, yl, zl), F32),
            pltpu.SemaphoreType.DMA((both,)),
        ],
        flops=1000000,
        moved=4 * zl * both * lanes,
        room=53.5,
        where=(HBM, VMEM),
    )
    mine, got = exchange(packed, nx, ny, [small])
    ring = []
    while sum(ring) < HALO:
        ring.append(min(zc, HALO - sum(ring)))
    block = (2, nx, ny * fields, lanes)
    unified = call(
        functools.partial(unify_kernel, nx, fields, ring),
        [((zc,) + block, F32)] + [((n,) + block, F32) for n in ring for _ in range(2)],
        [mine, got],
        flops=1000000,
        moved=8 * zl * both * lanes,
    )
    own, ends = unified[0], unified[1:]
    total = nz * chunks

    def ring_step(value, move):
        pairs = []
        for k in range(total):
            t = (k + move) % total
            pairs.append(((k % chunks) * nz + k // chunks, (t % chunks) * nz + t // chunks))
        return lax.ppermute(value, ("gx", "gy", "gz"), pairs)

    above = [ring_step(ends[2 * s], -(s + 1)) for s in range(len(ring))]
    below = [ring_step(ends[2 * s + 1], s + 1) for s in range(len(ring))]

    inner = list(range(2, half - 2))
    outer = [p for p in range(half) if p not in inner] + [EXTRA]

    def stencil(inputs, first_state, planes, kept, last):
        zz = sum(v.shape[0] for v in inputs)
        size = ((zz,) + block[1:], F32)
        outs = [((len(planes), 3 * 2 * ny * fields, nx * lanes), BF16)]
        outs += [((ny, zc * fields, lanes), F32)] * nx if last else [size] * 3
        return call(
            functools.partial(
                stencil_kernel,
                nx,
                ny,
                fields,
                yl,
                len(inputs),
                first_state,
                planes,
                bool(kept) or not last,
                last,
            ),
            outs,
            [*inputs, *kept],
            [pltpu.VMEM((zz,) + block, F32), pltpu.VMEM((zz, 7) + block[1:], F32)]
            + ([pltpu.VMEM(*size)] * 3 if last else []),
            flops=300000000,
            moved=8 * zz * nx * 8 * lanes,
            room=16 * (nx // 4) ** 2,
        )

    step = 2 if per_plane <= 256 else 1

    def attention(filtered, planes, more, outs, last):
        args = [
            filtered,
            sel,
            lift_w,
            small,
            query_weight,
            key_weight,
            value_weight,
            output_weight,
            up_weight,
            down_weight,
            head_w,
        ] + more
        size = (-(-len(planes) // step), 8, per_plane)
        work = len(planes) * per_plane * channels * (8 * channels + 4 * hidden) * 2
        return call(
            functools.partial(
                attention_kernel, nx, ny, fields, (xc, yc), step, last, bool(last and inner)
            ),
            outs if last else [(size, F32)],
            args,
            ([pltpu.VMEM(size, F32)] if last else []),
            flops=3 * work,
            moved=1000000,
            room=16 * (nx // 4) ** 2,
        )

    place = {}
    depth = 0
    for planes in (inner, outer):
        for i, p in enumerate(planes):
            place[p] = depth + (i // step) * 8 + (i % step) * fields
        depth += -(-len(planes) // step) * 8
    depth = -(-depth // 16) * 16

    more, kept = [], []
    if inner:
        filtered, *kept = stencil([own], 0, inner, [], False)
        more = list(attention(filtered, inner, [], None, False))

    ordered = below[::-1] + [own] + above
    second = stencil(ordered, HALO, outer, kept, True)
    filtered, state_messages = second[0], list(second[1:])

    width = -(-(xc + 2) * (yc + 2) // 128) * 128
    near = 128 // (xc * yc)
    spread = jnp.asarray(spread_matrix(ny, near, xc, yc, width), BF16)
    rows = zc * fields
    messages = attention(
        filtered,
        outer,
        more + [spread] + state_messages,
        [((ny, 2 * rows + depth, width), BF16)] * nx,
        True,
    )
    mine, got = exchange(list(messages), nx, ny)
    along_z = jnp.asarray(along_z_matrix(chunks, depth, place, fields, zc), BF16)
    across = jnp.asarray(across_matrix(xl, yl, width), BF16)
    state_next, eddy_field = call(
        functools.partial(return_kernel, nx, ny),
        [(flow_state.shape, F32)] * 2,
        [mine, got, along_z, across],
        [
            pltpu.VMEM((zl * fields, lanes), F32),
            pltpu.VMEM((chunks, depth, width), BF16),
            pltpu.VMEM(flow_state.shape, F32),
            pltpu.VMEM(flow_state.shape, F32),
            pltpu.SemaphoreType.DMA((2 * fields,)),
        ],
        flops=1000000,
        moved=8 * zl * fields * lanes,
        where=(VMEM, HBM),
    )
    return (state_next, eddy_field)


def solution(mesh):
    sizes = [mesh.shape[name] for name in ("gx", "gy", "gz")]
    return jax.shard_map(
        functools.partial(per_device, *sizes),
        mesh=mesh,
        in_specs=(
            P(None, "gx", "gy", "gz"),
            P(None, "gx", "gy", "gz"),
            P(),
            P(),
            P(),
            P(),
            P(),
            P(),
            P(),
            P(),
            P(),
            P(),
        ),
        out_specs=(P(None, "gx", "gy", "gz"), P(None, "gx", "gy", "gz")),
        check_vma=False,
    )
```

```python
import functools
import math

import jax
import jax.numpy as jnp
import numpy as np
from jax import lax
from jax.experimental import pallas as pl
from jax.experimental.pallas import tpu as pltpu
from jax.sharding import PartitionSpec as P

EPSILON = 1e-06
TIME_STEP = 0.3
HALO = 5
EXTRA = 1000
MASKED = -1e30
MIDDLE, REACH, OCTAVES = 0.275, 0.225, 118.0
F32 = jnp.float32
BF16 = jnp.bfloat16
VMEM = pl.BlockSpec(memory_space=pltpu.VMEM)
HBM = pl.BlockSpec(memory_space=pltpu.HBM)


def call(body, outs, args, scratch=(), flops=0, moved=0, room=16, where=(VMEM, VMEM)):
    return pl.pallas_call(
        body,
        out_shape=tuple(jax.ShapeDtypeStruct(s, d) for s, d in outs),
        in_specs=[where[0]] * len(args),
        out_specs=tuple([where[1]] * len(outs)),
        scratch_shapes=list(scratch),
        cost_estimate=pl.CostEstimate(flops=flops, bytes_accessed=moved, transcendentals=0),
        compiler_params=pltpu.CompilerParams(vmem_limit_bytes=int(min(room, 63.93) * 1048576)),
    )(*args)


def chunk_of(nx, ny, a, b, slab):
    if nx & (nx - 1) == 0:
        a = a ^ (a >> 1)
    chunk = a * ny + b
    return chunk + slab % 2 * (nx * ny - 1 - 2 * chunk)


def iota(shape, dim):
    return lax.broadcasted_iota(jnp.int32, shape, dim)


def halves(v):
    high = v.astype(BF16)
    return high, (v - high.astype(F32)).astype(BF16)


def coded(nu):
    place = (nu - MIDDLE) * (OCTAVES / REACH)
    size = jnp.exp2(2.0 * jnp.abs(place) - OCTAVES)
    return jnp.where(place < 0.0, -size, size).astype(BF16)


def decoded(code):
    size = (jnp.log2(jnp.abs(code)) + OCTAVES) * (0.5 * REACH / OCTAVES)
    return MIDDLE + jnp.where(code < 0.0, -size, size)


def pack_kernel(nx, ny, flow, visc, *rest):
    outs, (turned, blocks, sems) = rest[:nx], rest[nx:]
    fields, xl, yl, zl = flow.shape
    lanes = xl * yl
    both = 2 * fields
    copies = []
    for f in range(both):
        source = flow.at[f] if f < fields else visc.at[f - fields]
        copies.append(pltpu.make_async_copy(source, blocks.at[f], sems.at[f]))
        copies[f].start()
    for f in range(both):
        copies[f].wait()
        kind, row = divmod(f, fields)
        turned[kind, pl.ds(row, zl, stride=fields), :] = blocks[f].reshape(lanes, zl).T
    rows = zl * fields // (nx * ny)
    a, b = lax.axis_index("gx"), lax.axis_index("gy")
    slab = lax.axis_index("gz")
    for d in range(nx):
        for e in range(ny):
            chunk = chunk_of(nx, ny, lax.rem(a + d, nx), lax.rem(b + e, ny), slab)
            start = pl.multiple_of(chunk * rows, 8)
            high, low = halves(turned[0, pl.ds(start, rows), :])
            outs[d][e, 0] = high
            outs[d][e, 1] = low
            outs[d][e, 2] = coded(turned[1, pl.ds(start, rows), :])


def small_kernel(ny, fields, lift, bias, gains, head, small, lift_w, head_w):
    channels = gains.shape[1]
    small[:6] = gains[...] * channels**0.5
    small[6:7] = bias[...]
    small[7:8] = bias[...]
    rest = lift[...]
    rows = rest.shape[0]
    upper = lax.rem(iota((rows, channels), 0), 2 * fields) < fields
    for part in range(3):
        rounded = rest.astype(BF16)
        rest = rest - rounded.astype(F32)
        exact = rounded.astype(F32)
        swapped = pltpu.roll(exact, fields, 0)
        for b in range(ny):
            first = exact if b == 0 else swapped
            second = swapped if b == 0 else exact
            keep = upper if b == 0 else jnp.logical_not(upper)
            both = jnp.concatenate(
                [jnp.where(keep, first, 0.0), jnp.where(keep, second, 0.0)], axis=0
            ).astype(BF16)
            for again in range(3):
                at = (part * 3 + again) * 2 * rows
                lift_w[at : at + 2 * rows, b * channels : (b + 1) * channels] = both
    turned = head[...].astype(F32).T
    turned = jnp.concatenate([turned, jnp.zeros_like(turned)], axis=0)
    head_w[0] = turned.astype(BF16)
    head_w[1] = pltpu.roll(turned, fields, 0).astype(BF16)


def sort_kernel(nx, *refs):
    parts, (mine, away) = refs[:nx], refs[-2:]
    for d in range(nx):
        mine[d] = parts[d][0]
        away[d] = parts[d][1]


def unify_kernel(nx, fields, ring, mine, got, whole, *ends):
    a, b = lax.axis_index("gx"), lax.axis_index("gy")
    rows, lanes = got.shape[2:]
    zc = rows // fields
    shape = zc // 2, 2 * fields, lanes
    low = iota(shape, 1) < fields
    first = jnp.full(shape, b) == 0
    for d in range(nx):
        where_from = lax.rem(a + nx - d, nx)
        near = mine[d].astype(F32)
        far = got[d].astype(F32)
        for kind in range(2):
            m = (decoded(near[2]) if kind else near[0] + near[1]).reshape(shape)
            t = (decoded(far[2]) if kind else far[0] + far[1]).reshape(shape)
            p = jnp.where(first, m, t)
            q = jnp.where(first, t, m)
            even = jnp.where(low, p, pltpu.roll(q, fields, 1))
            odd = jnp.where(low, pltpu.roll(p, fields, 1), q)
            for z in range(zc // 2):
                whole[2 * z, kind, where_from] = even[z]
                whole[2 * z + 1, kind, where_from] = odd[z]
    for s, count in enumerate(ring):
        ends[2 * s][...] = whole[:count]
        ends[2 * s + 1][...] = whole[zc - count :]


class Shifts:
    def __init__(self, shape, yl, fields):
        self.lanes, self.yl, self.fields = shape[-1], yl, fields
        lane = iota(shape, 2)
        self.last_x = lane >= self.lanes - yl
        self.first_x = lane < yl
        inner = lax.rem(lane, yl)
        self.last_y = inner == yl - 1
        self.first_y = inner == 0

    def pairs(self, v):
        n, yl = self.lanes, self.yl
        r = pltpu.roll(v, n - yl, 2)
        xp = jnp.where(self.last_x, jnp.concatenate([r[1:], r[:1]], 0), r)
        r = pltpu.roll(v, yl, 2)
        xm = jnp.where(self.first_x, jnp.concatenate([r[-1:], r[:-1]], 0), r)
        other = pltpu.roll(v, self.fields, 1)
        yp = jnp.where(self.last_y, pltpu.roll(other, yl - 1, 2), pltpu.roll(v, n - 1, 2))
        ym = jnp.where(self.first_y, pltpu.roll(other, n - yl + 1, 2), pltpu.roll(v, 1, 2))
        return xp, xm, yp, ym


def stencil_kernel(nx, ny, fields, yl, blocks, first_state, planes, inner, outer, *refs):
    ins, refs = refs[:blocks], refs[blocks:]
    kept = ()
    if outer and inner:
        kept, refs = refs[:3], refs[3:]
    filtered, refs = refs[0], refs[1:]
    if outer:
        outs, refs = refs[:nx], refs[nx:]
        whole, coef, one, two, three = refs
    else:
        one, two, three, whole, coef = refs
    position = 0
    for ref in ins:
        count = ref.shape[0]
        whole[position : position + count] = ref[...]
        position += count
    zz = position
    zc = zz - 2 * first_state
    shape = whole.shape[2:]
    lanes = shape[-1]
    shifts = Shifts(shape, yl, fields)
    upper = iota(shape, 1) < fields

    def planes_of(margin):
        due = range(margin, zz - margin)
        if kept:
            own = range(first_state + margin, first_state + zc - margin)
            due = [z for z in due if z not in own]
        due = sorted(due, key=lambda z: min(z, zz - 1 - z))
        return due

    for z in sorted({z for margin in (1, 2, 3) for z in planes_of(margin)}):
        nu = whole[z, 1]
        total = None
        for k, other in enumerate((*shifts.pairs(nu), whole[z + 1, 1], whole[z - 1, 1])):
            face = nu + other
            coef[z, k] = face
            total = face if total is None else total + face
        coef[z, 6] = 1.0 - (0.5 * TIME_STEP) * total

    def advanced(load, row, z):
        c = load(z)
        xp, xm, yp, ym = shifts.pairs(c)
        total = None
        for d, (p, m) in enumerate(((xp, xm), (yp, ym), (load(z + 1), load(z - 1)))):
            top = jnp.broadcast_to(row(z, d), shape)
            velocity = jnp.where(upper, top, jnp.broadcast_to(row(z, fields + d), shape))
            term = (coef[z, 2 * d] - velocity) * p + (coef[z, 2 * d + 1] + velocity) * m
            total = term if total is None else total + term
        return c * coef[z, 6] + (0.5 * TIME_STEP) * total

    for z in planes_of(1):
        one[z] = advanced(lambda i: whole[i, 0], lambda i, r: whole[i, 0, :, r : r + 1, :], z)
    if kept:
        for z in (1, 2, zc - 3, zc - 2):
            one[first_state + z] = kept[0][z]
        for z in (2, 3, zc - 4, zc - 3):
            two[first_state + z] = kept[1][z]
        three[first_state + 3 : first_state + zc - 3] = kept[2][3 : zc - 3]
    for z in planes_of(2):
        moved = advanced(lambda i: one[i], lambda i, r: one[i, :, r : r + 1, :], z)
        two[z] = 0.75 * whole[z, 0] + 0.25 * moved
    for z in planes_of(3):
        moved = advanced(lambda i: two[i], lambda i, r: two[i, :, r : r + 1, :], z)
        three[z] = whole[z, 0] * (1.0 / 3.0) + (2.0 / 3.0) * moved

    if outer:
        a, b = lax.axis_index("gx"), lax.axis_index("gy")
        mask = iota((zc // 2, 2 * fields, lanes), 1) < fields
        first = jnp.full((zc // 2, 2 * fields, lanes), b) == 0
        for d in range(nx):
            target = lax.rem(a + d, nx)
            block = three[first_state : first_state + zc, target]
            block = block.reshape(zc // 2, 2, 2 * fields, lanes)
            even, odd = block[:, 0], block[:, 1]
            zero = jnp.where(mask, even, pltpu.roll(odd, fields, 1))
            other = jnp.where(mask, pltpu.roll(even, fields, 1), odd)
            outs[d][0] = jnp.where(first, zero, other).reshape(zc * fields, lanes)
            outs[d][1] = jnp.where(first, other, zero).reshape(zc * fields, lanes)

    chunk = chunk_of(nx, ny, *(lax.axis_index(name) for name in ("gx", "gy", "gz")))
    for i, plane in enumerate(planes):
        z = first_state + 2 * plane
        if plane == EXTRA:
            z = first_state + jnp.where(chunk < nx * ny // 2, -2, zc)
        s0, s1 = three[z], three[z + 1]
        rows = []
        for value in (s0 + s1, s0 * s0 + s1 * s1):
            value = value + pltpu.roll(value, lanes - yl, 2)
            rows.append(value + pltpu.roll(value, lanes - 1, 2))
        both = jnp.concatenate(rows, axis=1)
        height = both.shape[1]
        for part in range(3):
            rounded = both.astype(BF16)
            both = both - rounded.astype(F32)
            for k in range(shape[0]):
                filtered[
                    i, part * height : (part + 1) * height, k * lanes : (k + 1) * lanes
                ] = rounded[k]


def twice_gelu(x):
    inner = x * (0.7978845608028654 + 0.035677408136300125 * (x * x))
    return x + x * jnp.tanh(inner)


def rms_scale(v, gain):
    total = jnp.sum(v * v, axis=-1, keepdims=True)
    return v * lax.rsqrt(total + EPSILON * v.shape[-1]) * gain


def matmul(v, w):
    return jnp.dot(v, w, preferred_element_type=F32)


def against(v, w):
    return lax.dot_general(v, w, (((1,), (1,)), ((), ())), preferred_element_type=F32)


def attend(section, groups, same, weights, gain):
    qkv_w, out_w = weights
    channels = section.shape[1]
    carried = section.astype(F32)
    normed = rms_scale(carried, gain).astype(BF16)
    yield
    qkv = matmul(normed, qkv_w).astype(BF16)
    yield
    scale = channels ** (-0.5) * 1.4426950408889634
    values, scores = [], []
    for group in groups:
        rows = jnp.concatenate([qkv[s : s + n] for s, n in group], axis=0)
        q, k = rows[:, :channels], rows[:, channels : 2 * channels]
        values.append(rows[:, 2 * channels :])
        scores.append(jnp.where(same, against(q, k), MASKED))
        yield
    weighted = []
    for score in scores:
        exponent = jnp.exp2((score - jnp.max(score, axis=-1, keepdims=True)) * scale)
        weighted.append(exponent.astype(BF16))
        yield
    pieces = {}
    for group, exponent, v in zip(groups, weighted, values):
        summed = matmul(exponent, jnp.concatenate([v, jnp.ones_like(v)], axis=1))
        result = (summed[:, :channels] * (1.0 / summed[:, channels:])).astype(BF16)
        at = 0
        for s, n in group:
            pieces[s] = result[at : at + n]
            at += n
        yield
    attended = jnp.concatenate([pieces[s] for s in sorted(pieces)], axis=0)
    return carried + matmul(attended, out_w)


def feed(residual, weights, gain):
    up_w, down_w = weights
    again = rms_scale(residual, gain).astype(BF16)
    yield
    rows, hidden = residual.shape[0], up_w.shape[1]
    wide, tall = min(256, hidden), min(64, rows)
    total = None
    for h in range(0, hidden, wide):
        up = matmul(again, up_w[:, h : h + wide])
        pieces = []
        for r in range(0, rows, tall):
            pieces.append(twice_gelu(up[r : r + tall].astype(BF16)))
            yield
        down = matmul(jnp.concatenate(pieces, axis=0), down_w[h : h + wide])
        total = down if total is None else total + down
        yield
    return (residual + 0.5 * total).astype(BF16)


def together(tasks):
    results = [None] * len(tasks)
    alive = dict(enumerate(tasks))
    while alive:
        for i in list(alive):
            try:
                next(alive[i])
            except StopIteration as stop:
                results[i] = stop.value
                del alive[i]
    return results


def attention_kernel(nx, ny, fields, cells, step, last, earlier, *refs):
    filtered, sel, lift_w, gains, query_w, key_w, value_w = refs[:7]
    (out_w, up_w, down_w, head), refs = refs[7:11], refs[11:]
    if last:
        if earlier:
            before, refs = refs[0], refs[1:]
        spread, refs = refs[0], refs[1:]
        states, refs = refs[:nx], refs[nx:]
        outs, refs = refs[:nx], refs[nx:]
    coefficient = refs[0]
    xc, yc = cells
    channels = gains.shape[1]
    bias = gains[6:7]
    planes, height, wide = filtered.shape
    side = nx * xc * yc
    per_plane = ny * side
    cut, span = sel.shape
    along_x = [[(b * side, side)] for b in range(ny)]
    count = max(1, 128 // (ny * xc * yc))
    piece = count * xc * yc
    along_y = [
        [(b * side + g * piece, piece) for b in range(ny)] for g in range(nx // count)
    ]
    row, column = iota((side, side), 0), iota((side, side), 1)
    same_x_line = lax.rem(row, yc) == lax.rem(column, yc)
    count = ny * piece
    row, column = iota((count, count), 0), iota((count, count), 1)
    same_y_line = lax.rem(row, piece) // yc == lax.rem(column, piece) // yc
    gain = [gains[i : i + 1] for i in range(6)]
    qkv_w = [
        jnp.concatenate([query_w[i], key_w[i], value_w[i]], axis=1) for i in range(2)
    ]

    def lift_and_first(block):
        by_core = [[] for _ in range(ny)]
        for g in range(wide // span):
            parts = block[:, g * span : (g + 1) * span]
            picked = against(sel[...], jnp.concatenate([parts] * 3, axis=0)).astype(BF16)
            yield
            both = matmul(picked, lift_w[...])
            for b in range(ny):
                by_core[b].append(both[:, b * channels : (b + 1) * channels])
        yield
        features = []
        for rows in sum(by_core, []):
            lifted = rows + bias
            features.append((0.5 * twice_gelu(rms_scale(lifted, gain[0]))).astype(BF16))
            yield
        features = jnp.concatenate(features, axis=0)
        weights = qkv_w[0], out_w[0]
        return (yield from attend(features, along_x, same_x_line, weights, gain[1]))

    def first_feed(residual):
        return feed(residual, (up_w[0], down_w[0]), gain[2])

    def second(value):
        return attend(value, along_y, same_y_line, (qkv_w[1], out_w[1]), gain[3])

    def second_feed_and_head(residual, turned, plus):
        value = yield from feed(residual, (up_w[1], down_w[1]), gain[4])
        final = rms_scale(value.astype(F32), gain[5]).astype(BF16)
        yield
        logits = against(turned, final)
        return logits if plus is None else logits + plus

    def coefficient_of(logits):
        return 0.05 + 0.45 * jax.nn.sigmoid(logits)

    def chain(plane, turned):
        value = yield from lift_and_first(plane)
        value = yield from first_feed(value)
        value = yield from second(value)
        return (yield from second_feed_and_head(value, turned, None))

    def some_planes(i, carry):
        tasks = [chain(filtered[i * width + p], head[p % step]) for p in range(width)]
        found = together(tasks)
        for p in range(0, width, step):
            row = i * (width // step) + p // step
            coefficient[row] = coefficient_of(sum(found[p + 1 : p + step], found[p]))
        return carry

    width = planes if planes * per_plane <= 2048 else step
    lax.fori_loop(0, planes // width, some_planes, 0)

    if last:
        a, b = lax.axis_index("gx"), lax.axis_index("gy")
        every = coefficient[...].reshape(-1, per_plane)
        if earlier:
            every = jnp.concatenate([before[...].reshape(-1, per_plane), every], axis=0)
        kept = 2 * states[0].shape[1]
        depth = outs[0].shape[1] - kept
        if every.shape[0] < depth:
            blank = jnp.zeros((depth - every.shape[0], per_plane), F32)
            every = jnp.concatenate([every, blank], axis=0)
        every = every.astype(BF16).astype(F32)
        width = spread.shape[1] // ny
        first = jnp.full((depth, width), b) == 0
        for d in range(nx):
            target = lax.rem(a + d, nx)
            shift = lax.rem((nx + 1 - target) * (xc * yc), side)
            near = [
                pltpu.roll(every[:, k * side : (k + 1) * side], shift, 1)[:, :cut]
                for k in range(ny)
            ]
            near = jnp.concatenate(near, axis=1).astype(BF16)
            found = matmul(near, spread[...])
            zero, other = found[:, :width], found[:, width:]
            high, low = halves(states[d][...])
            outs[d][:, : kept // 2] = high
            outs[d][:, kept // 2 : kept] = low
            outs[d][0, kept:] = jnp.where(first, zero, other).astype(BF16)
            outs[d][1, kept:] = jnp.where(first, other, zero).astype(BF16)


def return_kernel(nx, ny, mine, got, along_z, across, *refs):
    state_out, eddy_out, state_rows, coarse_rows, state, eddy, sems = refs
    fields, xl, yl, zl = state_out.shape
    a, b = lax.axis_index("gx"), lax.axis_index("gy")
    slab = lax.axis_index("gz")
    size = state_rows.shape[0] // (nx * ny)
    for d in range(nx):
        for piece, core in ((mine, b), (got, lax.rem(b + 1, ny))):
            chunk = chunk_of(nx, ny, lax.rem(a + nx - d, nx), core, slab)
            start = pl.multiple_of(chunk * size, 8)
            high, low = piece[d, :size].astype(F32), piece[d, size : 2 * size].astype(F32)
            state_rows[pl.ds(start, size), :] = high + low
            coarse_rows[chunk] = piece[d, 2 * size :]
    copies = []

    def send(buffer, out, f):
        copy = pltpu.make_async_copy(buffer.at[f], out.at[f], sems.at[len(copies)])
        copy.start()
        copies.append(copy)

    for f in range(fields):
        rows = state_rows[pl.ds(f, zl, stride=fields), :]
        state[f] = rows.T.reshape(xl, yl, zl)
        send(state, state_out, f)
    count, depth, width = coarse_rows.shape
    coarse = coarse_rows[...].reshape(count * depth, width)
    for f in range(fields):
        spread = lax.dot_general(
            coarse,
            along_z[:, f * zl : (f + 1) * zl],
            (((0,), (0,)), ((), ())),
            preferred_element_type=F32,
        )
        total = None
        for part in range(3):
            rounded = spread.astype(BF16)
            spread = spread - rounded.astype(F32)
            product = matmul(across[...], rounded)
            total = product if total is None else total + product
        eddy[f] = total.reshape(xl, yl, zl)
        send(eddy, eddy_out, f)
    for copy in copies:
        copy.wait()


def pick_matrix(group, xl, yl):
    xc, yc = xl // 2, yl // 2
    table = np.zeros((group, xl, yl, group, xc, yc), np.float32)
    for k in range(group):
        for x in range(xc):
            for y in range(yc):
                table[k, 2 * x, 2 * y, k, x, y] = 0.125
    return table.reshape(group * xl * yl, group * xc * yc)


def spread_matrix(ny, near, xc, yc, width):
    table = np.zeros((ny, near, xc, yc, ny, width), np.float32)
    for target in range(ny):
        for i in range(xc + 2):
            x = i - 1 + xc
            for j in range(yc + 2):
                y = (target * yc + j - 1) % (ny * yc)
                table[y // yc, x // xc, x % xc, y % yc, target, i * (yc + 2) + j] = 1.0
    return table.reshape(ny * near * xc * yc, ny * width)


def taps(fine):
    return ((fine // 2, 0.75), (fine // 2 + (1 if fine % 2 else -1), 0.25))


def across_matrix(xl, yl, width):
    yc = yl // 2
    table = np.zeros((xl, yl, width), np.float32)
    for x in range(xl):
        for y in range(yl):
            for i, u in taps(x):
                for j, v in taps(y):
                    table[x, y, (i + 1) * (yc + 2) + j + 1] += u * v
    return table.reshape(xl * yl, width)


def along_z_matrix(chunks, depth, place, fields, zc):
    half = zc // 2
    table = np.zeros((chunks, depth, fields, chunks * zc), np.float32)
    for z in range(chunks * zc):
        for i, u in taps(z):
            if 0 <= i < chunks * half:
                c, row = i // half, place[i % half]
            else:
                c, row = (0 if i < 0 else chunks - 1), place[EXTRA]
            for f in range(fields):
                table[c, row + f, f, z] += u
    return table.reshape(chunks * depth, fields * chunks * zc)


def exchange(messages, nx, ny, meanwhile=()):
    received = [messages[0]] + [None] * (nx - 1)
    for d in sorted(range(1, nx), key=lambda d: abs(2 * d - nx)):
        received[d] = lax.ppermute(messages[d], "gx", [(i, (i + d) % nx) for i in range(nx)])
    shape = (nx,) + messages[0].shape[1:]
    mine, away = call(
        functools.partial(sort_kernel, nx),
        [(shape, messages[0].dtype)] * 2,
        [*received, *meanwhile],
        flops=1000,
        moved=8 * math.prod(shape),
    )
    return mine, lax.ppermute(away, "gy", [(i, (i + 1) % ny) for i in range(ny)])


def per_device(
    nx,
    ny,
    nz,
    flow_state,
    viscosity,
    lift_weight,
    lift_bias,
    norm_gains,
    query_weight,
    key_weight,
    value_weight,
    output_weight,
    up_weight,
    down_weight,
    head_weight,
):
    fields, xl, yl, zl = flow_state.shape
    lanes = xl * yl
    chunks = nx * ny
    zc = zl // chunks
    half = zc // 2
    xc, yc = xl // 2, yl // 2
    channels = lift_bias.shape[0]
    hidden = up_weight.shape[-1]
    both = 2 * fields
    per_plane = chunks * xc * yc

    group = max(1, 512 // lanes)
    sel = jnp.asarray(pick_matrix(group, xl, yl).T, BF16)
    small, lift_w, head_w = call(
        functools.partial(small_kernel, ny, fields),
        [
            ((8, channels), F32),
            ((9 * 2 * ny * fields, ny * channels), BF16),
            ((2, 8, channels), BF16),
        ],
        [lift_weight, lift_bias.reshape(1, channels), norm_gains, head_weight],
        flops=1000000,
        moved=200000,
    )

    packed = call(
        functools.partial(pack_kernel, nx, ny),
        [((ny, 3, zc * fields, lanes), BF16)] * nx,
        [flow_state, viscosity],
        [
            pltpu.VMEM((2, zl * fields, lanes), F32),
            pltpu.VMEM((both, xl, yl, zl), F32),
            pltpu.SemaphoreType.DMA((both,)),
        ],
        flops=1000000,
        moved=4 * zl * both * lanes,
        room=53.5,
        where=(HBM, VMEM),
    )
    mine, got = exchange(packed, nx, ny, [small])
    ring = []
    while sum(ring) < HALO:
        ring.append(min(zc, HALO - sum(ring)))
    block = (2, nx, ny * fields, lanes)
    unified = call(
        functools.partial(unify_kernel, nx, fields, ring),
        [((zc,) + block, F32)] + [((n,) + block, F32) for n in ring for _ in range(2)],
        [mine, got],
        flops=1000000,
        moved=8 * zl * both * lanes,
    )
    own, ends = unified[0], unified[1:]
    total = nz * chunks

    devices = {}
    for a in range(nx):
        for b in range(ny):
            for slab in range(nz):
                position = slab * chunks + chunk_of(nx, ny, a, b, slab)
                devices[position] = (a * ny + b) * nz + slab

    def ring_step(value, move):
        pairs = [(devices[k], devices[(k + move) % total]) for k in range(total)]
        return lax.ppermute(value, ("gx", "gy", "gz"), pairs)

    above = [ring_step(ends[2 * s], -(s + 1)) for s in range(len(ring))]
    below = [ring_step(ends[2 * s + 1], s + 1) for s in range(len(ring))]

    inner = list(range(2, half - 2))
    outer = [p for p in range(half) if p not in inner] + [EXTRA]

    def stencil(inputs, first_state, planes, kept, last):
        zz = sum(v.shape[0] for v in inputs)
        size = ((zz,) + block[1:], F32)
        outs = [((len(planes), 3 * 2 * ny * fields, nx * lanes), BF16)]
        outs += [((ny, zc * fields, lanes), F32)] * nx if last else [size] * 3
        return call(
            functools.partial(
                stencil_kernel,
                nx,
                ny,
                fields,
                yl,
                len(inputs),
                first_state,
                planes,
                bool(kept) or not last,
                last,
            ),
            outs,
            [*inputs, *kept],
            [pltpu.VMEM((zz,) + block, F32), pltpu.VMEM((zz, 7) + block[1:], F32)]
            + ([pltpu.VMEM(*size)] * 3 if last else []),
            flops=300000000,
            moved=8 * zz * nx * 8 * lanes,
            room=16 * (nx // 4) ** 2,
        )

    step = 2 if per_plane <= 256 else 1

    def attention(filtered, planes, more, outs, last):
        args = [
            filtered,
            sel,
            lift_w,
            small,
            query_weight,
            key_weight,
            value_weight,
            output_weight,
            up_weight,
            down_weight,
            head_w,
        ] + more
        size = (-(-len(planes) // step), 8, per_plane)
        work = len(planes) * per_plane * channels * (8 * channels + 4 * hidden) * 2
        return call(
            functools.partial(
                attention_kernel, nx, ny, fields, (xc, yc), step, last, bool(last and inner)
            ),
            outs if last else [(size, F32)],
            args,
            ([pltpu.VMEM(size, F32)] if last else []),
            flops=3 * work,
            moved=1000000,
            room=16 * (nx // 4) ** 2,
        )

    place = {}
    depth = 0
    for planes in (inner, outer):
        for i, p in enumerate(planes):
            place[p] = depth + (i // step) * 8 + (i % step) * fields
        depth += -(-len(planes) // step) * 8
    depth = -(-depth // 16) * 16

    more, kept = [], []
    if inner:
        filtered, *kept = stencil([own], 0, inner, [], False)
        more = list(attention(filtered, inner, [], None, False))

    ordered = below[::-1] + [own] + above
    second = stencil(ordered, HALO, outer, kept, True)
    filtered, state_messages = second[0], list(second[1:])

    width = -(-(xc + 2) * (yc + 2) // 128) * 128
    near = 128 // (xc * yc)
    spread = jnp.asarray(spread_matrix(ny, near, xc, yc, width), BF16)
    rows = zc * fields
    messages = attention(
        filtered,
        outer,
        more + [spread] + state_messages,
        [((ny, 2 * rows + depth, width), BF16)] * nx,
        True,
    )
    mine, got = exchange(list(messages), nx, ny)
    along_z = jnp.asarray(along_z_matrix(chunks, depth, place, fields, zc), BF16)
    across = jnp.asarray(across_matrix(xl, yl, width), BF16)
    state_next, eddy_field = call(
        functools.partial(return_kernel, nx, ny),
        [(flow_state.shape, F32)] * 2,
        [mine, got, along_z, across],
        [
            pltpu.VMEM((zl * fields, lanes), F32),
            pltpu.VMEM((chunks, depth, width), BF16),
            pltpu.VMEM(flow_state.shape, F32),
            pltpu.VMEM(flow_state.shape, F32),
            pltpu.SemaphoreType.DMA((2 * fields,)),
        ],
        flops=1000000,
        moved=8 * zl * fields * lanes,
        where=(VMEM, HBM),
    )
    return (state_next, eddy_field)


def solution(mesh):
    sizes = [mesh.shape[name] for name in ("gx", "gy", "gz")]
    return jax.shard_map(
        functools.partial(per_device, *sizes),
        mesh=mesh,
        in_specs=(
            P(None, "gx", "gy", "gz"),
            P(None, "gx", "gy", "gz"),
            P(),
            P(),
            P(),
            P(),
            P(),
            P(),
            P(),
            P(),
            P(),
            P(),
        ),
        out_specs=(P(None, "gx", "gy", "gz"), P(None, "gx", "gy", "gz")),
        check_vma=False,
    )
```

```python
import functools
import math

import jax
import jax.numpy as jnp
import numpy as np
from jax import lax
from jax.experimental import pallas as pl
from jax.experimental.pallas import tpu as pltpu
from jax.sharding import PartitionSpec as P

EPSILON = 1e-06
TIME_STEP = 0.3
HALO = 5
EXTRA = 1000
MASKED = -1e30
MIDDLE, REACH, OCTAVES = 0.275, 0.225, 118.0
LOWEST, SPAN = -45.0, 64.0
F32 = jnp.float32
BF16 = jnp.bfloat16
VMEM = pl.BlockSpec(memory_space=pltpu.VMEM)
HBM = pl.BlockSpec(memory_space=pltpu.HBM)


def call(body, outs, args, scratch=(), flops=0, moved=0, room=16, where=(VMEM, VMEM)):
    return pl.pallas_call(
        body,
        out_shape=tuple(jax.ShapeDtypeStruct(s, d) for s, d in outs),
        in_specs=[where[0]] * len(args),
        out_specs=tuple([where[1]] * len(outs)),
        scratch_shapes=list(scratch),
        cost_estimate=pl.CostEstimate(flops=flops, bytes_accessed=moved, transcendentals=0),
        compiler_params=pltpu.CompilerParams(vmem_limit_bytes=int(min(room, 63.93) * 1048576)),
    )(*args)


def chunk_of(nx, ny, a, b, slab):
    if nx & (nx - 1) == 0:
        a = a ^ (a >> 1)
    chunk = a * ny + b
    return chunk + slab % 2 * (nx * ny - 1 - 2 * chunk)


def iota(shape, dim):
    return lax.broadcasted_iota(jnp.int32, shape, dim)


def halves(v):
    high = v.astype(BF16)
    return high, (v - high.astype(F32)).astype(BF16)


def coded(nu):
    place = (nu - MIDDLE) * (OCTAVES / REACH)
    size = jnp.exp2(2.0 * jnp.abs(place) - OCTAVES)
    return jnp.where(place < 0.0, -size, size).astype(BF16)


def decoded(code):
    size = (jnp.log2(jnp.abs(code)) + OCTAVES) * (0.5 * REACH / OCTAVES)
    return MIDDLE + jnp.where(code < 0.0, -size, size)


def coded_state(v):
    place = jnp.log2(jnp.maximum(jnp.abs(v), 2.0**LOWEST)) - LOWEST
    size = jnp.exp2(place * (2.0 * OCTAVES / SPAN) - OCTAVES)
    return jnp.where(v < 0.0, -size, size).astype(BF16)


def decoded_state(code):
    place = (jnp.log2(jnp.abs(code)) + OCTAVES) * (0.5 * SPAN / OCTAVES)
    size = jnp.where(place < 0.0005, 0.0, jnp.exp2(place + LOWEST))
    return jnp.where(code < 0.0, -size, size)


def pack_kernel(nx, ny, flow, visc, *rest):
    outs, (turned, blocks, sems) = rest[:nx], rest[nx:]
    fields, xl, yl, zl = flow.shape
    lanes = xl * yl
    both = 2 * fields
    copies = []
    for f in range(both):
        source = flow.at[f] if f < fields else visc.at[f - fields]
        copies.append(pltpu.make_async_copy(source, blocks.at[f], sems.at[f]))
        copies[f].start()
    for f in range(both):
        copies[f].wait()
        kind, row = divmod(f, fields)
        turned[kind, pl.ds(row, zl, stride=fields), :] = blocks[f].reshape(lanes, zl).T
    rows = zl * fields // (nx * ny)
    a, b = lax.axis_index("gx"), lax.axis_index("gy")
    slab = lax.axis_index("gz")
    for d in range(nx):
        for e in range(ny):
            chunk = chunk_of(nx, ny, lax.rem(a + d, nx), lax.rem(b + e, ny), slab)
            start = pl.multiple_of(chunk * rows, 8)
            high, low = halves(turned[0, pl.ds(start, rows), :])
            outs[d][e, 0] = high
            outs[d][e, 1] = low
            outs[d][e, 2] = coded(turned[1, pl.ds(start, rows), :])


def small_kernel(ny, fields, lift, bias, gains, head, small, lift_w, head_w):
    channels = gains.shape[1]
    small[:6] = gains[...] * channels**0.5
    small[6:7] = bias[...]
    small[7:8] = bias[...]
    rest = lift[...]
    rows = rest.shape[0]
    upper = lax.rem(iota((rows, channels), 0), 2 * fields) < fields
    for part in range(3):
        rounded = rest.astype(BF16)
        rest = rest - rounded.astype(F32)
        exact = rounded.astype(F32)
        swapped = pltpu.roll(exact, fields, 0)
        for b in range(ny):
            first = exact if b == 0 else swapped
            second = swapped if b == 0 else exact
            keep = upper if b == 0 else jnp.logical_not(upper)
            both = jnp.concatenate(
                [jnp.where(keep, first, 0.0), jnp.where(keep, second, 0.0)], axis=0
            ).astype(BF16)
            for again in range(3):
                at = (part * 3 + again) * 2 * rows
                lift_w[at : at + 2 * rows, b * channels : (b + 1) * channels] = both
    turned = head[...].astype(F32).T
    turned = jnp.concatenate([turned, jnp.zeros_like(turned)], axis=0)
    head_w[0] = turned.astype(BF16)
    head_w[1] = pltpu.roll(turned, fields, 0).astype(BF16)


def sort_kernel(nx, *refs):
    parts, (mine, away) = refs[:nx], refs[-2:]
    for d in range(nx):
        mine[d] = parts[d][0]
        away[d] = parts[d][1]


def unify_kernel(nx, fields, ring, mine, got, whole, *ends):
    a, b = lax.axis_index("gx"), lax.axis_index("gy")
    rows, lanes = got.shape[2:]
    zc = rows // fields
    shape = zc // 2, 2 * fields, lanes
    low = iota(shape, 1) < fields
    first = jnp.full(shape, b) == 0
    for d in range(nx):
        where_from = lax.rem(a + nx - d, nx)
        near = mine[d].astype(F32)
        far = got[d].astype(F32)
        for kind in range(2):
            m = (decoded(near[2]) if kind else near[0] + near[1]).reshape(shape)
            t = (decoded(far[2]) if kind else far[0] + far[1]).reshape(shape)
            p = jnp.where(first, m, t)
            q = jnp.where(first, t, m)
            even = jnp.where(low, p, pltpu.roll(q, fields, 1))
            odd = jnp.where(low, pltpu.roll(p, fields, 1), q)
            for z in range(zc // 2):
                whole[2 * z, kind, where_from] = even[z]
                whole[2 * z + 1, kind, where_from] = odd[z]
    for s, count in enumerate(ring):
        ends[2 * s][...] = whole[:count]
        ends[2 * s + 1][...] = whole[zc - count :]


class Shifts:
    def __init__(self, shape, yl, fields):
        self.lanes, self.yl, self.fields = shape[-1], yl, fields
        lane = iota(shape, 2)
        self.last_x = lane >= self.lanes - yl
        self.first_x = lane < yl
        inner = lax.rem(lane, yl)
        self.last_y = inner == yl - 1
        self.first_y = inner == 0

    def pairs(self, v):
        n, yl = self.lanes, self.yl
        r = pltpu.roll(v, n - yl, 2)
        xp = jnp.where(self.last_x, jnp.concatenate([r[1:], r[:1]], 0), r)
        r = pltpu.roll(v, yl, 2)
        xm = jnp.where(self.first_x, jnp.concatenate([r[-1:], r[:-1]], 0), r)
        other = pltpu.roll(v, self.fields, 1)
        yp = jnp.where(self.last_y, pltpu.roll(other, yl - 1, 2), pltpu.roll(v, n - 1, 2))
        ym = jnp.where(self.first_y, pltpu.roll(other, n - yl + 1, 2), pltpu.roll(v, 1, 2))
        return xp, xm, yp, ym


def stencil_kernel(nx, ny, fields, yl, blocks, first_state, planes, inner, outer, *refs):
    ins, refs = refs[:blocks], refs[blocks:]
    kept = ()
    if outer and inner:
        kept, refs = refs[:3], refs[3:]
    filtered, refs = refs[0], refs[1:]
    if outer:
        outs, refs = refs[:nx], refs[nx:]
        whole, coef, one, two, three = refs
    else:
        one, two, three, whole, coef = refs
    position = 0
    for ref in ins:
        count = ref.shape[0]
        whole[position : position + count] = ref[...]
        position += count
    zz = position
    zc = zz - 2 * first_state
    shape = whole.shape[2:]
    lanes = shape[-1]
    shifts = Shifts(shape, yl, fields)
    upper = iota(shape, 1) < fields

    def planes_of(margin):
        due = range(margin, zz - margin)
        if kept:
            own = range(first_state + margin, first_state + zc - margin)
            due = [z for z in due if z not in own]
        due = sorted(due, key=lambda z: min(z, zz - 1 - z))
        return due

    for z in sorted({z for margin in (1, 2, 3) for z in planes_of(margin)}):
        nu = whole[z, 1]
        total = None
        for k, other in enumerate((*shifts.pairs(nu), whole[z + 1, 1], whole[z - 1, 1])):
            face = nu + other
            coef[z, k] = face
            total = face if total is None else total + face
        coef[z, 6] = 1.0 - (0.5 * TIME_STEP) * total

    def advanced(load, row, z):
        c = load(z)
        xp, xm, yp, ym = shifts.pairs(c)
        total = None
        for d, (p, m) in enumerate(((xp, xm), (yp, ym), (load(z + 1), load(z - 1)))):
            top = jnp.broadcast_to(row(z, d), shape)
            velocity = jnp.where(upper, top, jnp.broadcast_to(row(z, fields + d), shape))
            term = (coef[z, 2 * d] - velocity) * p + (coef[z, 2 * d + 1] + velocity) * m
            total = term if total is None else total + term
        return c * coef[z, 6] + (0.5 * TIME_STEP) * total

    for z in planes_of(1):
        one[z] = advanced(lambda i: whole[i, 0], lambda i, r: whole[i, 0, :, r : r + 1, :], z)
    if kept:
        for z in (1, 2, zc - 3, zc - 2):
            one[first_state + z] = kept[0][z]
        for z in (2, 3, zc - 4, zc - 3):
            two[first_state + z] = kept[1][z]
        three[first_state + 3 : first_state + zc - 3] = kept[2][3 : zc - 3]
    for z in planes_of(2):
        moved = advanced(lambda i: one[i], lambda i, r: one[i, :, r : r + 1, :], z)
        two[z] = 0.75 * whole[z, 0] + 0.25 * moved
    for z in planes_of(3):
        moved = advanced(lambda i: two[i], lambda i, r: two[i, :, r : r + 1, :], z)
        three[z] = whole[z, 0] * (1.0 / 3.0) + (2.0 / 3.0) * moved

    if outer:
        a, b = lax.axis_index("gx"), lax.axis_index("gy")
        mask = iota((zc // 2, 2 * fields, lanes), 1) < fields
        first = jnp.full((zc // 2, 2 * fields, lanes), b) == 0
        for d in range(nx):
            target = lax.rem(a + d, nx)
            block = three[first_state : first_state + zc, target]
            block = block.reshape(zc // 2, 2, 2 * fields, lanes)
            even, odd = block[:, 0], block[:, 1]
            zero = jnp.where(mask, even, pltpu.roll(odd, fields, 1))
            other = jnp.where(mask, pltpu.roll(even, fields, 1), odd)
            outs[d][0] = jnp.where(first, zero, other).reshape(zc * fields, lanes)
            outs[d][1] = jnp.where(first, other, zero).reshape(zc * fields, lanes)

    chunk = chunk_of(nx, ny, *(lax.axis_index(name) for name in ("gx", "gy", "gz")))
    for i, plane in enumerate(planes):
        z = first_state + 2 * plane
        if plane == EXTRA:
            z = first_state + jnp.where(chunk < nx * ny // 2, -2, zc)
        s0, s1 = three[z], three[z + 1]
        rows = []
        for value in (s0 + s1, s0 * s0 + s1 * s1):
            value = value + pltpu.roll(value, lanes - yl, 2)
            rows.append(value + pltpu.roll(value, lanes - 1, 2))
        both = jnp.concatenate(rows, axis=1)
        height = both.shape[1]
        for part in range(3):
            rounded = both.astype(BF16)
            both = both - rounded.astype(F32)
            for k in range(shape[0]):
                filtered[
                    i, part * height : (part + 1) * height, k * lanes : (k + 1) * lanes
                ] = rounded[k]


def twice_gelu(x):
    inner = x * (0.7978845608028654 + 0.035677408136300125 * (x * x))
    return x + x * jnp.tanh(inner)


def rms_scale(v, gain):
    total = jnp.sum(v * v, axis=-1, keepdims=True)
    return v * lax.rsqrt(total + EPSILON * v.shape[-1]) * gain


def matmul(v, w):
    return jnp.dot(v, w, preferred_element_type=F32)


def against(v, w):
    return lax.dot_general(v, w, (((1,), (1,)), ((), ())), preferred_element_type=F32)


def attend(section, groups, same, weights, gain):
    qkv_w, out_w = weights
    channels = section.shape[1]
    carried = section.astype(F32)
    normed = rms_scale(carried, gain).astype(BF16)
    yield
    qkv = matmul(normed, qkv_w).astype(BF16)
    yield
    scale = channels ** (-0.5) * 1.4426950408889634
    values, scores = [], []
    for group in groups:
        rows = jnp.concatenate([qkv[s : s + n] for s, n in group], axis=0)
        q, k = rows[:, :channels], rows[:, channels : 2 * channels]
        values.append(rows[:, 2 * channels :])
        scores.append(jnp.where(same, against(q, k), MASKED))
        yield
    weighted = []
    for score in scores:
        exponent = jnp.exp2((score - jnp.max(score, axis=-1, keepdims=True)) * scale)
        weighted.append(exponent.astype(BF16))
        yield
    pieces = {}
    for group, exponent, v in zip(groups, weighted, values):
        summed = matmul(exponent, jnp.concatenate([v, jnp.ones_like(v)], axis=1))
        result = (summed[:, :channels] * (1.0 / summed[:, channels:])).astype(BF16)
        at = 0
        for s, n in group:
            pieces[s] = result[at : at + n]
            at += n
        yield
    attended = jnp.concatenate([pieces[s] for s in sorted(pieces)], axis=0)
    return carried + matmul(attended, out_w)


def feed(residual, weights, gain):
    up_w, down_w = weights
    again = rms_scale(residual, gain).astype(BF16)
    yield
    rows, hidden = residual.shape[0], up_w.shape[1]
    wide, tall = min(256, hidden), min(64, rows)
    total = None
    for h in range(0, hidden, wide):
        up = matmul(again, up_w[:, h : h + wide])
        pieces = []
        for r in range(0, rows, tall):
            pieces.append(twice_gelu(up[r : r + tall].astype(BF16)))
            yield
        down = matmul(jnp.concatenate(pieces, axis=0), down_w[h : h + wide])
        total = down if total is None else total + down
        yield
    return (residual + 0.5 * total).astype(BF16)


def together(tasks):
    results = [None] * len(tasks)
    alive = dict(enumerate(tasks))
    while alive:
        for i in list(alive):
            try:
                next(alive[i])
            except StopIteration as stop:
                results[i] = stop.value
                del alive[i]
    return results


def attention_kernel(nx, ny, fields, cells, step, last, earlier, *refs):
    filtered, sel, lift_w, gains, query_w, key_w, value_w = refs[:7]
    (out_w, up_w, down_w, head), refs = refs[7:11], refs[11:]
    if last:
        if earlier:
            before, refs = refs[0], refs[1:]
        spread, refs = refs[0], refs[1:]
        states, refs = refs[:nx], refs[nx:]
        outs, refs = refs[:nx], refs[nx:]
    coefficient = refs[0]
    xc, yc = cells
    channels = gains.shape[1]
    bias = gains[6:7]
    planes, height, wide = filtered.shape
    side = nx * xc * yc
    per_plane = ny * side
    cut, span = sel.shape
    along_x = [[(b * side, side)] for b in range(ny)]
    count = max(1, 128 // (ny * xc * yc))
    piece = count * xc * yc
    along_y = [
        [(b * side + g * piece, piece) for b in range(ny)] for g in range(nx // count)
    ]
    row, column = iota((side, side), 0), iota((side, side), 1)
    same_x_line = lax.rem(row, yc) == lax.rem(column, yc)
    count = ny * piece
    row, column = iota((count, count), 0), iota((count, count), 1)
    same_y_line = lax.rem(row, piece) // yc == lax.rem(column, piece) // yc
    gain = [gains[i : i + 1] for i in range(6)]
    qkv_w = [
        jnp.concatenate([query_w[i], key_w[i], value_w[i]], axis=1) for i in range(2)
    ]

    def lift_and_first(block):
        by_core = [[] for _ in range(ny)]
        for g in range(wide // span):
            parts = block[:, g * span : (g + 1) * span]
            picked = against(sel[...], jnp.concatenate([parts] * 3, axis=0)).astype(BF16)
            yield
            both = matmul(picked, lift_w[...])
            for b in range(ny):
                by_core[b].append(both[:, b * channels : (b + 1) * channels])
        yield
        features = []
        for rows in sum(by_core, []):
            lifted = rows + bias
            features.append((0.5 * twice_gelu(rms_scale(lifted, gain[0]))).astype(BF16))
            yield
        features = jnp.concatenate(features, axis=0)
        weights = qkv_w[0], out_w[0]
        return (yield from attend(features, along_x, same_x_line, weights, gain[1]))

    def first_feed(residual):
        return feed(residual, (up_w[0], down_w[0]), gain[2])

    def second(value):
        return attend(value, along_y, same_y_line, (qkv_w[1], out_w[1]), gain[3])

    def second_feed_and_head(residual, turned, plus):
        value = yield from feed(residual, (up_w[1], down_w[1]), gain[4])
        final = rms_scale(value.astype(F32), gain[5]).astype(BF16)
        yield
        logits = against(turned, final)
        return logits if plus is None else logits + plus

    def coefficient_of(logits):
        return 0.05 + 0.45 * jax.nn.sigmoid(logits)

    def chain(plane, turned):
        value = yield from lift_and_first(plane)
        value = yield from first_feed(value)
        value = yield from second(value)
        return (yield from second_feed_and_head(value, turned, None))

    def some_planes(i, carry):
        tasks = [chain(filtered[i * width + p], head[p % step]) for p in range(width)]
        found = together(tasks)
        for p in range(0, width, step):
            row = i * (width // step) + p // step
            coefficient[row] = coefficient_of(sum(found[p + 1 : p + step], found[p]))
        return carry

    width = planes if planes * per_plane <= 2048 else step
    lax.fori_loop(0, planes // width, some_planes, 0)

    if last:
        a, b = lax.axis_index("gx"), lax.axis_index("gy")
        every = coefficient[...].reshape(-1, per_plane)
        if earlier:
            every = jnp.concatenate([before[...].reshape(-1, per_plane), every], axis=0)
        kept = states[0].shape[1]
        depth = outs[0].shape[1] - kept
        if every.shape[0] < depth:
            blank = jnp.zeros((depth - every.shape[0], per_plane), F32)
            every = jnp.concatenate([every, blank], axis=0)
        every = every.astype(BF16).astype(F32)
        width = spread.shape[1] // ny
        first = jnp.full((depth, width), b) == 0
        for d in range(nx):
            target = lax.rem(a + d, nx)
            shift = lax.rem((nx + 1 - target) * (xc * yc), side)
            near = [
                pltpu.roll(every[:, k * side : (k + 1) * side], shift, 1)[:, :cut]
                for k in range(ny)
            ]
            near = jnp.concatenate(near, axis=1).astype(BF16)
            found = matmul(near, spread[...])
            zero, other = found[:, :width], found[:, width:]
            outs[d][:, :kept] = coded_state(states[d][...])
            outs[d][0, kept:] = jnp.where(first, zero, other).astype(BF16)
            outs[d][1, kept:] = jnp.where(first, other, zero).astype(BF16)


def return_kernel(nx, ny, mine, got, along_z, across, *refs):
    state_out, eddy_out, state_rows, coarse_rows, state, eddy, sems = refs
    fields, xl, yl, zl = state_out.shape
    a, b = lax.axis_index("gx"), lax.axis_index("gy")
    slab = lax.axis_index("gz")
    size = state_rows.shape[0] // (nx * ny)
    for d in range(nx):
        for piece, core in ((mine, b), (got, lax.rem(b + 1, ny))):
            chunk = chunk_of(nx, ny, lax.rem(a + nx - d, nx), core, slab)
            start = pl.multiple_of(chunk * size, 8)
            state_rows[pl.ds(start, size), :] = decoded_state(piece[d, :size].astype(F32))
            coarse_rows[chunk] = piece[d, size:]
    copies = []

    def send(buffer, out, f):
        copy = pltpu.make_async_copy(buffer.at[f], out.at[f], sems.at[len(copies)])
        copy.start()
        copies.append(copy)

    for f in range(fields):
        rows = state_rows[pl.ds(f, zl, stride=fields), :]
        state[f] = rows.T.reshape(xl, yl, zl)
        send(state, state_out, f)
    count, depth, width = coarse_rows.shape
    coarse = coarse_rows[...].reshape(count * depth, width)
    for f in range(fields):
        spread = lax.dot_general(
            coarse,
            along_z[:, f * zl : (f + 1) * zl],
            (((0,), (0,)), ((), ())),
            preferred_element_type=F32,
        )
        total = None
        for part in range(3):
            rounded = spread.astype(BF16)
            spread = spread - rounded.astype(F32)
            product = matmul(across[...], rounded)
            total = product if total is None else total + product
        eddy[f] = total.reshape(xl, yl, zl)
        send(eddy, eddy_out, f)
    for copy in copies:
        copy.wait()


def pick_matrix(group, xl, yl):
    xc, yc = xl // 2, yl // 2
    table = np.zeros((group, xl, yl, group, xc, yc), np.float32)
    for k in range(group):
        for x in range(xc):
            for y in range(yc):
                table[k, 2 * x, 2 * y, k, x, y] = 0.125
    return table.reshape(group * xl * yl, group * xc * yc)


def spread_matrix(ny, near, xc, yc, width):
    table = np.zeros((ny, near, xc, yc, ny, width), np.float32)
    for target in range(ny):
        for i in range(xc + 2):
            x = i - 1 + xc
            for j in range(yc + 2):
                y = (target * yc + j - 1) % (ny * yc)
                table[y // yc, x // xc, x % xc, y % yc, target, i * (yc + 2) + j] = 1.0
    return table.reshape(ny * near * xc * yc, ny * width)


def taps(fine):
    return ((fine // 2, 0.75), (fine // 2 + (1 if fine % 2 else -1), 0.25))


def across_matrix(xl, yl, width):
    yc = yl // 2
    table = np.zeros((xl, yl, width), np.float32)
    for x in range(xl):
        for y in range(yl):
            for i, u in taps(x):
                for j, v in taps(y):
                    table[x, y, (i + 1) * (yc + 2) + j + 1] += u * v
    return table.reshape(xl * yl, width)


def along_z_matrix(chunks, depth, place, fields, zc):
    half = zc // 2
    table = np.zeros((chunks, depth, fields, chunks * zc), np.float32)
    for z in range(chunks * zc):
        for i, u in taps(z):
            if 0 <= i < chunks * half:
                c, row = i // half, place[i % half]
            else:
                c, row = (0 if i < 0 else chunks - 1), place[EXTRA]
            for f in range(fields):
                table[c, row + f, f, z] += u
    return table.reshape(chunks * depth, fields * chunks * zc)


def exchange(messages, nx, ny, meanwhile=()):
    received = [messages[0]] + [None] * (nx - 1)
    for d in sorted(range(1, nx), key=lambda d: abs(2 * d - nx)):
        received[d] = lax.ppermute(messages[d], "gx", [(i, (i + d) % nx) for i in range(nx)])
    shape = (nx,) + messages[0].shape[1:]
    mine, away = call(
        functools.partial(sort_kernel, nx),
        [(shape, messages[0].dtype)] * 2,
        [*received, *meanwhile],
        flops=1000,
        moved=8 * math.prod(shape),
    )
    return mine, lax.ppermute(away, "gy", [(i, (i + 1) % ny) for i in range(ny)])


def per_device(
    nx,
    ny,
    nz,
    flow_state,
    viscosity,
    lift_weight,
    lift_bias,
    norm_gains,
    query_weight,
    key_weight,
    value_weight,
    output_weight,
    up_weight,
    down_weight,
    head_weight,
):
    fields, xl, yl, zl = flow_state.shape
    lanes = xl * yl
    chunks = nx * ny
    zc = zl // chunks
    half = zc // 2
    xc, yc = xl // 2, yl // 2
    channels = lift_bias.shape[0]
    hidden = up_weight.shape[-1]
    both = 2 * fields
    per_plane = chunks * xc * yc

    group = max(1, 512 // lanes)
    sel = jnp.asarray(pick_matrix(group, xl, yl).T, BF16)
    small, lift_w, head_w = call(
        functools.partial(small_kernel, ny, fields),
        [
            ((8, channels), F32),
            ((9 * 2 * ny * fields, ny * channels), BF16),
            ((2, 8, channels), BF16),
        ],
        [lift_weight, lift_bias.reshape(1, channels), norm_gains, head_weight],
        flops=1000000,
        moved=200000,
    )

    packed = call(
        functools.partial(pack_kernel, nx, ny),
        [((ny, 3, zc * fields, lanes), BF16)] * nx,
        [flow_state, viscosity],
        [
            pltpu.VMEM((2, zl * fields, lanes), F32),
            pltpu.VMEM((both, xl, yl, zl), F32),
            pltpu.SemaphoreType.DMA((both,)),
        ],
        flops=1000000,
        moved=4 * zl * both * lanes,
        room=53.5,
        where=(HBM, VMEM),
    )
    mine, got = exchange(packed, nx, ny, [small])
    ring = []
    while sum(ring) < HALO:
        ring.append(min(zc, HALO - sum(ring)))
    block = (2, nx, ny * fields, lanes)
    unified = call(
        functools.partial(unify_kernel, nx, fields, ring),
        [((zc,) + block, F32)] + [((n,) + block, F32) for n in ring for _ in range(2)],
        [mine, got],
        flops=1000000,
        moved=8 * zl * both * lanes,
    )
    own, ends = unified[0], unified[1:]
    total = nz * chunks

    devices = {}
    for a in range(nx):
        for b in range(ny):
            for slab in range(nz):
                position = slab * chunks + chunk_of(nx, ny, a, b, slab)
                devices[position] = (a * ny + b) * nz + slab

    def ring_step(value, move):
        pairs = [(devices[k], devices[(k + move) % total]) for k in range(total)]
        return lax.ppermute(value, ("gx", "gy", "gz"), pairs)

    above = [ring_step(ends[2 * s], -(s + 1)) for s in range(len(ring))]
    below = [ring_step(ends[2 * s + 1], s + 1) for s in range(len(ring))]

    inner = list(range(2, half - 2))
    outer = [p for p in range(half) if p not in inner] + [EXTRA]

    def stencil(inputs, first_state, planes, kept, last):
        zz = sum(v.shape[0] for v in inputs)
        size = ((zz,) + block[1:], F32)
        outs = [((len(planes), 3 * 2 * ny * fields, nx * lanes), BF16)]
        outs += [((ny, zc * fields, lanes), F32)] * nx if last else [size] * 3
        return call(
            functools.partial(
                stencil_kernel,
                nx,
                ny,
                fields,
                yl,
                len(inputs),
                first_state,
                planes,
                bool(kept) or not last,
                last,
            ),
            outs,
            [*inputs, *kept],
            [pltpu.VMEM((zz,) + block, F32), pltpu.VMEM((zz, 7) + block[1:], F32)]
            + ([pltpu.VMEM(*size)] * 3 if last else []),
            flops=300000000,
            moved=8 * zz * nx * 8 * lanes,
            room=16 * (nx // 4) ** 2,
        )

    step = 2 if per_plane <= 256 else 1

    def attention(filtered, planes, more, outs, last):
        args = [
            filtered,
            sel,
            lift_w,
            small,
            query_weight,
            key_weight,
            value_weight,
            output_weight,
            up_weight,
            down_weight,
            head_w,
        ] + more
        size = (-(-len(planes) // step), 8, per_plane)
        work = len(planes) * per_plane * channels * (8 * channels + 4 * hidden) * 2
        return call(
            functools.partial(
                attention_kernel, nx, ny, fields, (xc, yc), step, last, bool(last and inner)
            ),
            outs if last else [(size, F32)],
            args,
            ([pltpu.VMEM(size, F32)] if last else []),
            flops=3 * work,
            moved=1000000,
            room=16 * (nx // 4) ** 2,
        )

    place = {}
    depth = 0
    for planes in (inner, outer):
        for i, p in enumerate(planes):
            place[p] = depth + (i // step) * 8 + (i % step) * fields
        depth += -(-len(planes) // step) * 8
    depth = -(-depth // 16) * 16

    more, kept = [], []
    if inner:
        filtered, *kept = stencil([own], 0, inner, [], False)
        more = list(attention(filtered, inner, [], None, False))

    ordered = below[::-1] + [own] + above
    second = stencil(ordered, HALO, outer, kept, True)
    filtered, state_messages = second[0], list(second[1:])

    width = -(-(xc + 2) * (yc + 2) // 128) * 128
    near = 128 // (xc * yc)
    spread = jnp.asarray(spread_matrix(ny, near, xc, yc, width), BF16)
    rows = zc * fields
    messages = attention(
        filtered,
        outer,
        more + [spread] + state_messages,
        [((ny, rows + depth, width), BF16)] * nx,
        True,
    )
    mine, got = exchange(list(messages), nx, ny)
    along_z = jnp.asarray(along_z_matrix(chunks, depth, place, fields, zc), BF16)
    across = jnp.asarray(across_matrix(xl, yl, width), BF16)
    state_next, eddy_field = call(
        functools.partial(return_kernel, nx, ny),
        [(flow_state.shape, F32)] * 2,
        [mine, got, along_z, across],
        [
            pltpu.VMEM((zl * fields, lanes), F32),
            pltpu.VMEM((chunks, depth, width), BF16),
            pltpu.VMEM(flow_state.shape, F32),
            pltpu.VMEM(flow_state.shape, F32),
            pltpu.SemaphoreType.DMA((2 * fields,)),
        ],
        flops=1000000,
        moved=8 * zl * fields * lanes,
        where=(VMEM, HBM),
    )
    return (state_next, eddy_field)


def solution(mesh):
    sizes = [mesh.shape[name] for name in ("gx", "gy", "gz")]
    return jax.shard_map(
        functools.partial(per_device, *sizes),
        mesh=mesh,
        in_specs=(
            P(None, "gx", "gy", "gz"),
            P(None, "gx", "gy", "gz"),
            P(),
            P(),
            P(),
            P(),
            P(),
            P(),
            P(),
            P(),
            P(),
            P(),
        ),
        out_specs=(P(None, "gx", "gy", "gz"), P(None, "gx", "gy", "gz")),
        check_vma=False,
    )
```
